32 devices in a mesh: sector: 4 (over x, core), op: 8 (over z, y).
Axes of the slice: x: 2, y: 2, z: 4, core: 2. Of those that a mesh axis runs over, the one named last changes fastest.
Arguments:
- wavefunction: bfloat16 [8, 512, 512], P('sector', 'op'), may hold values from -6 to 6
- sector_bases: bfloat16 [8, 512, 512], P('sector', 'op'), may hold values from -1 to 1
- left_env: bfloat16 [192, 512, 512], P(('sector', 'op')), may hold values from -0.25 to 0.25
- right_env: bfloat16 [192, 512, 512], P(('sector', 'op')), may hold values from -0.0546875 to 0.0546875
- pair_source: int32 [192], P(('sector', 'op')), may hold values from 0 to 7, as said below
- pair_target: int32 [192], P(('sector', 'op')), may hold values from 0 to 7
- sector_slot: int32 [8], replicated, may hold values from 0 to 7, as said below
- orders: int32 [8], replicated, may hold values from 256 to 512, as said below
Outputs:
- sigma_blocks: bfloat16 [8, 512, 512], P('sector', 'op')
- left_rotated: bfloat16 [192, 512, 512], P(('sector', 'op'))
The draws below stay inside these ranges and needn't reach their ends.
Inputs may be any that keep to these rules, and one draw needn't show every extreme that they name: A permutation: sector s's blocks stand at slot sector_slot[s]. `pair_source`: the pairs held by index i of the sector axis have sources whose slots lie in i * 2 to (i + 1) * 2 - 1. `orders`: some sector has order exactly 512.
All inputs are finite; a program needn't handle non-finite values.
Results may differ from the reference program's by a relative error of at most 0.0049.
Values may be sent and summed in bfloat16 or wider, within the bound.
A program may use at most 128 MiB of HBM per device.

```python
import jax
import jax.numpy as jnp
from jax import lax

K = 512
SEC_DEV = 2
PAIRS_DEV = 6
SECTORS = 8
PAIRS = 192
N_SECTOR = 4
N_OP = 8


def slot_table(key):
    return jax.random.permutation(jax.random.fold_in(key, 11), SECTORS).astype(jnp.int32)


def draw_sector_slot(key, part):
    return slot_table(key)


def draw_pair_source(key, part):
    table = slot_table(key)
    sector_of = jnp.argsort(table, stable=True).astype(jnp.int32)
    numbers = jnp.arange(PAIRS, dtype=jnp.int32)
    owner_ids = numbers // (PAIRS // N_SECTOR)
    picks = jax.random.randint(jax.random.fold_in(key, 12), (PAIRS,), 0, SEC_DEV, dtype=jnp.int32)
    return sector_of[owner_ids * SEC_DEV + picks]


def draw_orders(key, part):
    base = jax.random.randint(jax.random.fold_in(key, 14), (SECTORS,), K // 2, K + 1, dtype=jnp.int32)
    marked = jax.random.randint(jax.random.fold_in(key, 15), (), 0, SECTORS, dtype=jnp.int32)
    labels = jnp.arange(SECTORS, dtype=jnp.int32)
    return jnp.where(labels == marked, K, base).astype(jnp.int32)


def plant(drawn, rng, low, largest):
    index_at = [jax.random.randint(jax.random.fold_in(rng, axis), (), 0, length) for axis, length in enumerate(drawn.shape)]
    main_axis = drawn.shape.index(max(drawn.shape))
    neighbour = index_at[:main_axis] + [(index_at[main_axis] + 1) % drawn.shape[main_axis]] + index_at[main_axis + 1:]
    return drawn.at[tuple(index_at)].set(low).at[tuple(neighbour)].set(largest)


def steps_of(stream_key, shape, pieces, low, top_value):
    def one(position, parts):
        heights = jax.random.uniform(jax.random.fold_in(jax.random.fold_in(stream_key, 6), position), (parts,), jnp.float32, low / len(pieces), top_value / len(pieces))
        return jnp.repeat(jnp.exp(heights), shape[position] // parts).reshape((-1,) + (1,) * (len(shape) - position - 1))

    gain = one(*pieces[0])
    for cut in pieces[1:]:
        gain = gain * one(*cut)
    return gain


def gaussian(key, shape, spread, limit, pieces=(), kind=jnp.bfloat16):
    loudness = steps_of(key, shape, pieces, -0.22, 0.18) if pieces else 1.0
    values = jax.random.normal(key, shape, jnp.float32) * spread * loudness
    return jnp.minimum(jnp.maximum(values, -limit), limit).astype(kind)


def setup_inputs(seed: int = 0) -> dict:
    seeds = jax.random.split(jax.random.key(seed), 9)
    return {
        "wavefunction": gaussian(seeds[0], (SECTORS, K, K), 1.0, 6.0, ((0, 4), (1, 8))),
        "sector_bases": gaussian(seeds[1], (SECTORS, K, K), (K // 16) ** -0.5, 1.0, ((0, 4), (1, 8))),
        "left_env": gaussian(seeds[2], (PAIRS, K, K), K ** -0.5, 0.25, ((0, 32),)),
        "right_env": gaussian(seeds[3], (PAIRS, K, K), (K * PAIRS_DEV * N_OP // SEC_DEV) ** -0.5, 0.0546875, ((0, 32),)),
        "pair_source": draw_pair_source(jax.random.fold_in(seeds[8], 71), 0),
        "pair_target": plant(jax.random.randint(seeds[5], (PAIRS,), 0, SECTORS), jax.random.fold_in(seeds[5], 1), 0, SECTORS - 1).astype(jnp.int32),
        "sector_slot": draw_sector_slot(jax.random.fold_in(seeds[8], 71), 0),
        "orders": draw_orders(jax.random.fold_in(seeds[8], 71), 0),
    }


def reference(wavefunction, sector_bases, left_env, right_env, pair_source, pair_target, sector_slot, orders):
    sectors = orders.shape[0]
    width = wavefunction.shape[1]
    slot_order = jnp.zeros((sectors,), jnp.int32).at[sector_slot].set(orders)
    positions = jnp.arange(width, dtype=jnp.int32)
    edge = positions[None, :] < slot_order[:, None]
    inside = edge[:, :, None] & edge[:, None, :]
    masked = jnp.where(inside, wavefunction, jnp.zeros((), wavefunction.dtype))
    source_slot = sector_slot[pair_source].astype(jnp.int32)
    target_slot = sector_slot[pair_target].astype(jnp.int32)

    def apply_pair(totals, entry):
        left_block, right_block, source_at, target_at = entry
        projected = jnp.dot(left_block, masked[source_at], preferred_element_type=jnp.float32).astype(jnp.bfloat16)
        product = jnp.dot(projected, right_block.T, preferred_element_type=jnp.float32)
        totals = totals.at[target_at].add(product)
        half_rotated = jnp.dot(left_block, sector_bases[source_at], preferred_element_type=jnp.float32).astype(jnp.bfloat16)
        rotated = jnp.dot(sector_bases[target_at].T, half_rotated, preferred_element_type=jnp.float32).astype(jnp.bfloat16)
        return totals, rotated

    start_sum = jnp.zeros((sectors, width, width), jnp.float32)
    totals, left_rotated = lax.scan(apply_pair, start_sum, (left_env, right_env, source_slot, target_slot))
    sigma_blocks = jnp.where(inside, totals, jnp.zeros((), jnp.float32)).astype(jnp.bfloat16)
    return sigma_blocks, left_rotated
```

```python
import functools

import jax
import jax.numpy as jnp
from jax import lax
from jax.experimental import pallas as pl
from jax.experimental.pallas import tpu as pltpu
from jax.sharding import PartitionSpec as P

MESH = pl.DeviceIdType.MESH
ANY = pl.BlockSpec(memory_space=pl.ANY)
VMEM = pl.BlockSpec(memory_space=pltpu.VMEM)
SMEM = pl.BlockSpec(memory_space=pltpu.SMEM)


def grid_of(n_sector, n_op):
    cores = 2 if n_sector % 2 == 0 else 1
    ny = 1
    while ny * ny * 4 <= n_op and n_op % (ny * 2) == 0:
        ny *= 2
    return n_sector // cores, cores, n_op // ny, ny


class Place:
    def __init__(self, dims):
        self.dims = dims
        nx, nc, nz, ny = dims
        sector, op = lax.axis_index("sector"), lax.axis_index("op")
        self.x, self.c = sector // nc, sector % nc
        self.z, self.y = op // ny, op % ny

    def at(self, x=0, c=0, z=0, y=0):
        nx, nc, nz, ny = self.dims
        return (
            lax.rem(self.x + x, nx),
            lax.rem(self.c + c, nc),
            lax.rem(self.z + z, nz),
            lax.rem(self.y + y, ny),
        )

    def device(self, **shift):
        nx, nc, nz, ny = self.dims
        x, c, z, y = self.at(**shift)
        return (x * nc + c, z * ny + y)

    def greet(self):
        barrier = pltpu.get_barrier_semaphore()
        count = 0
        for name, n in zip("xczy", self.dims):
            for shift in range(1, n):
                pl.semaphore_signal(
                    barrier, inc=1, device_id=self.device(**{name: shift}), device_id_type=MESH
                )
                count += 1
        pl.semaphore_wait(barrier, count)


def remote(src, dst, send, recv, device):
    return pltpu.make_async_remote_copy(
        src_ref=src, dst_ref=dst, send_sem=send, recv_sem=recv, device_id=device, device_id_type=MESH
    )


def order_of(slot, sector_slot, orders, sectors):
    total = jnp.int32(0)
    for i in range(sectors):
        total = total + jnp.where(sector_slot[i] == slot, orders[i], 0)
    return total


def sigma_kernel(
    dims, sectors, wave_ref, base_ref, left_hbm, right_hbm, source, target, sector_slot, orders,
    out, rotated_hbm,
    wave_all, base_all, masked, own_bases, half, left, right, product,
    send_c, got_c, send_1, got_1, mid, send_2, got_2, held, send_3, got_3,
    local, give, wzs, wzr, wys, wyr, azs, azr, ays, ayr, axs, axr,
    bxs, bxr, bys, byr, bzs, bzr, kcs, kcr,
    cs, cr, s1, r1, s2, r2, s3, r3,
):
    nx, nc, nz, ny = dims
    me = Place(dims)
    per_owner, slab, width = out.shape
    count = left.shape[0]
    strip = ny * slab
    f32, bf16 = jnp.float32, jnp.bfloat16
    size = {"x": nx, "y": ny}
    first = (me.x * nc + me.c) * per_owner
    even = list(range(0, per_owner, 2))
    odd = list(range(1, per_owner, 2))

    def rows(z, y):
        return pl.ds((z * ny + y) * slab, slab)

    def wave(z, e=0):
        return wave_all.at[:, rows(z, lax.rem(me.y + ny - e, ny)), :]

    def slot_of(j, f, g=0):
        x, c, _, _ = me.at(x=nx - f, c=nc - g)
        return (x * nc + c) * per_owner + j

    def base(j, z, e=0, f=0):
        return base_all.at[slot_of(j, f), rows(z, lax.rem(me.y + ny - e, ny)), :]

    def base_strip(j, z, f, g=0):
        return base_all.at[slot_of(j, f, g), pl.ds(z * strip, strip), :]

    keep_wave = pltpu.make_async_copy(wave_ref, wave(me.z), local.at[0])
    keep_base = pltpu.make_async_copy(
        base_ref, base_all.at[pl.ds(first, per_owner), rows(me.z, me.y), :], local.at[1]
    )
    take_left = pltpu.make_async_copy(left_hbm, left, local.at[2])
    take_right = pltpu.make_async_copy(right_hbm, right, local.at[3])

    def chain(src, dst, send, recv, up):
        return remote(src, dst, send, recv, me.device(z=1 if up else nz - 1))

    def wave_z(up, z, src):
        return chain(src, wave(z), wzs.at[0 if up else 1, z], wzr.at[z], up)

    def wave_y(z, e, src):
        return remote(src, wave(z), wys.at[e, z], wyr.at[e, z], me.device(y=e))

    def a_z(j):
        def copy(up, z, src):
            return chain(src, base(j, z), azs.at[0 if up else 1, j, z], azr.at[j, z], up)

        return copy

    def a_y(j, z, e, src):
        return remote(src, base(j, z), ays.at[j, e, z], ayr.at[j, e, z], me.device(y=e))

    def a_x(j, z, e, f, src):
        return remote(src, base(j, z, e), axs.at[j, f, e, z], axr.at[j, f, e, z], me.device(x=f))

    def b_x(j, f, src):
        return remote(src, base(j, me.z), bxs.at[j, f], bxr.at[j, f], me.device(x=f))

    def b_y(j, f, e, src):
        return remote(src, base(j, me.z, 0, f), bys.at[j, f, e], byr.at[j, f, e], me.device(y=e))

    def b_z(j, f):
        def copy(up, z, src):
            return chain(
                src, base_strip(j, z, f), bzs.at[0 if up else 1, j, f, z], bzr.at[j, f, z], up
            )

        return copy

    def core(j, f, z):
        block = base_strip(j, z, f)
        return remote(block, block, kcs.at[j, f, z], kcr.at[j, f, z], me.device(c=1))

    def give_core(j, f, z):
        if nc > 1:
            core(j, f, z).start()

    def far_z(d, visit):
        @pl.when(me.z >= d)
        def _():
            visit(me.z - d, True)

        @pl.when(me.z + d < nz)
        def _():
            visit(me.z + d, False)

    def both_ways(start, src):
        @pl.when(me.z < nz - 1)
        def _():
            start(True, me.z, src).start()

        @pl.when(me.z > 0)
        def _():
            start(False, me.z, src).start()

    def relay(copy, block, z, up):
        copy(up, z, block).wait_recv()

        @pl.when(me.z < nz - 1 if up else me.z > 0)
        def _():
            copy(up, z, block).start()

    def sent_z(start, block):
        @pl.when(me.z < nz - 1)
        def _():
            @pl.loop(0, me.z + 1)
            def _(z):
                start(True, z, block(z)).wait_send()

        @pl.when(me.z > 0)
        def _():
            @pl.loop(me.z, nz)
            def _(z):
                start(False, z, block(z)).wait_send()

    me.greet()
    both_ways(wave_z, wave_ref)
    for e in range(1, ny):
        wave_y(me.z, e, wave_ref).start()
    for f in range(1, nx):
        for j in odd:
            b_x(j, f, base_ref.at[j]).start()
        for j in even:
            a_x(j, me.z, 0, f, base_ref.at[j]).start()
    keep_wave.start()
    keep_base.start()
    take_left.start()
    take_right.start()

    def on_wave(z, up):
        relay(wave_z, wave(z), z, up)
        for e in range(1, ny):
            wave_y(z, e, wave(z)).start()

    for d in range(1, nz):
        far_z(d, on_wave)
    for j in even:
        both_ways(a_z(j), base_ref.at[j])
    for e in range(1, ny):
        for j in odd:
            b_y(j, 0, e, base_ref.at[j]).start()
            for f in range(1, nx):
                if e == 1:
                    b_x(j, f, base(j, me.z, 0, f)).wait_recv()
                b_y(j, f, e, base(j, me.z, 0, f)).start()
        for j in even:
            a_y(j, me.z, e, base_ref.at[j]).start()

    def on_a(z, up):
        for j in even:
            block = base(j, z)
            relay(a_z(j), block, z, up)
            for e in range(1, ny):
                a_y(j, z, e, block).start()
            for f in range(1, nx):
                a_x(j, z, 0, f, block).start()

    def on_b_y(f):
        for j in odd:
            for e in range(1, ny):
                b_y(j, f, e, base(j, me.z, e, f)).wait_recv()
            block = base_strip(j, me.z, f)
            both_ways(b_z(j, f), block)
            give_core(j, f, me.z)

    def on_b(z, up):
        for j in odd:
            for f in range(nx):
                block = base_strip(j, z, f)
                relay(b_z(j, f), block, z, up)
                give_core(j, f, z)

    def on_a_y(i):
        z = lax.rem(me.z + i, nz)
        for j in even:
            for e in range(1, ny):
                block = base(j, z, e)
                a_y(j, z, e, block).wait_recv()
                for f in range(1, nx):
                    a_x(j, z, e, f, block).start()
            give_core(j, 0, z)

    def on_a_x(i):
        z = lax.rem(me.z + i, nz)
        for j in even:
            for f in range(1, nx):
                for e in range(ny):
                    a_x(j, z, e, f, base(j, z, e, f)).wait_recv()
                give_core(j, f, z)

    keep_wave.wait()
    keep_base.wait()
    take_left.wait()
    take_right.wait()
    for e in range(1, ny):

        @pl.loop(0, nz)
        def _(z):
            wave_y(z, e, wave(z, e)).wait_recv()

    row = lax.broadcasted_iota(jnp.int32, (width, width), 0)
    column = lax.broadcasted_iota(jnp.int32, (width, width), 1)
    for j in range(per_owner):
        order = order_of(first + j, sector_slot, orders, sectors)
        inside = jnp.maximum(row, column) < order
        masked[j] = jnp.where(inside, wave_all[j], jnp.zeros((), bf16))

    tasks = [functools.partial(far_z, d, on_a) for d in range(1, nz)]
    tasks += [functools.partial(on_b_y, f) for f in range(nx)]
    for p in range(count):
        a = lax.rem(sector_slot[source[p]], per_owner)
        projected = jnp.dot(left[p], masked[a], preferred_element_type=f32)
        product[p] = lax.dot_general(
            projected.astype(bf16), right[p], (((1,), (1,)), ((), ())),
            preferred_element_type=f32,
        )
        for task in tasks[p * len(tasks) // count : (p + 1) * len(tasks) // count]:
            task()

    landed = [sector_slot[target[p]] for p in range(count)]

    def partial_sum(slot, start, size):
        total = None
        for p in range(count):
            weight = jnp.where(landed[p] == slot, 1.0, 0.0).astype(f32)
            term = product[p, pl.ds(start, size), :] * weight
            total = term if total is None else total + term
        return total

    def axes(j):
        return ("x", "y") if j % 2 == 0 else ("y", "x")

    def zq(d):
        return lax.rem(me.z + d, nz)

    def core_copy(x, j, d):
        return remote(
            send_c.at[d, j, x], got_c.at[d, j, x], cs.at[d, j, x], cr.at[d, j, x], me.device(c=1)
        )

    def copy_1(j, d, k):
        return remote(
            send_1.at[d, j, k], got_1.at[d, j, k], s1.at[d, j, k], r1.at[d, j, k],
            me.device(**{axes(j)[0]: k}),
        )

    def copy_2(j, d, k):
        return remote(
            send_2.at[d, j, k], got_2.at[d, j, k], s2.at[d, j, k], r2.at[d, j, k],
            me.device(**{axes(j)[1]: k}),
        )

    def copy_3(j, d):
        return remote(
            send_3.at[d, j], got_3.at[d, j], s3.at[d, j], r3.at[d, j], me.device(z=d)
        )

    def stage_0(d):
        for j in range(per_owner):
            for x in range(nx):
                slot = (x * nc + lax.rem(me.c + 1, nc)) * per_owner + j
                for m in range(ny):
                    value = partial_sum(slot, pl.multiple_of(zq(d) * strip + m * slab, slab), slab)
                    send_c[d, j, x, pl.ds(m * slab, slab), :] = value.astype(bf16)
                core_copy(x, j, d).start()

    def stage_1(d):
        for j in range(per_owner):
            n1 = size[axes(j)[0]]
            n2 = size[axes(j)[1]]
            if nc > 1:
                for x in range(nx):
                    core_copy(x, j, d).wait_recv()
            for k in list(range(1, n1)) + [0]:
                for m in range(n2):
                    if axes(j)[0] == "x":
                        x, y = lax.rem(me.x + k, nx), m
                    else:
                        x, y = m, lax.rem(me.y + k, ny)
                    offset = pl.multiple_of(y * slab, slab)
                    slot = (x * nc + me.c) * per_owner + j
                    value = partial_sum(slot, pl.multiple_of(zq(d) * strip + offset, slab), slab)
                    if nc > 1:
                        value = value + got_c[d, j, x, pl.ds(offset, slab), :].astype(f32)
                    if k:
                        send_1[d, j, k, m] = value.astype(bf16)
                    else:
                        mid[d, j, m] = value
                if k:
                    copy_1(j, d, k).start()

    def stage_2(d):
        for j in range(per_owner):
            axis_1, axis_2 = axes(j)
            n1, n2 = size[axis_1], size[axis_2]
            for k in range(1, n1):
                copy_1(j, d, k).wait_recv()
            for h in list(range(1, n2)) + [0]:
                m = lax.rem(getattr(me, axis_2) + h, n2)
                value = mid[d, j, m]
                for k in range(1, n1):
                    value = value + got_1[d, j, k, m].astype(f32)
                if h:
                    send_2[d, j, h] = value.astype(bf16)
                    copy_2(j, d, h).start()
                else:
                    held[d, j] = value

    def stage_3(d, j):
        for h in range(1, size[axes(j)[1]]):
            copy_2(j, d, h).wait_recv()
        value = held[d, j]
        for h in range(1, size[axes(j)[1]]):
            value = value + got_2[d, j, h].astype(f32)
        return value

    def stage_3_send(d):
        for j in range(per_owner):
            send_3[d, j] = stage_3(d, j).astype(bf16)
            copy_3(j, d).start()

    take_bases = pltpu.make_async_copy(
        base_all.at[pl.ds(first, per_owner)], own_bases, local.at[4]
    )

    def rotate_half():
        take_bases.start()
        take_bases.wait()
        for p in range(count):
            a = lax.rem(sector_slot[source[p]], per_owner)
            half[p] = jnp.dot(left[p], own_bases[a], preferred_element_type=f32).astype(bf16)

    def give_rotated(p):
        return pltpu.make_async_copy(right.at[p], rotated_hbm.at[p], give.at[p])

    def rotate():
        if nc > 1:
            for j in range(per_owner):
                for f in range(nx):

                    @pl.loop(0, nz)
                    def _(z):
                        core(j, f, z).wait_recv()

        for p in range(count):
            right[p] = lax.dot_general(
                base_all[sector_slot[target[p]]], half[p], (((0,), (0,)), ((), ())),
                preferred_element_type=f32,
            ).astype(bf16)
            give_rotated(p).start()

    def sent_bases():
        sent_z(wave_z, wave)

        @pl.loop(0, nz)
        def _(z):
            for e in range(1, ny):
                wave_y(z, e, wave(z)).wait_send()
            for j in even:
                for e in range(1, ny):
                    a_y(j, z, e, base(j, z)).wait_send()
                for f in range(1, nx):
                    for e in range(ny):
                        a_x(j, z, e, f, base(j, z, e)).wait_send()

        for j in even:
            sent_z(a_z(j), functools.partial(base, j))
        for j in odd:
            for f in range(1, nx):
                b_x(j, f, base(j, me.z)).wait_send()
            for f in range(nx):
                for e in range(1, ny):
                    b_y(j, f, e, base(j, me.z, 0, f)).wait_send()

    @pl.loop(0, nz + 3)
    def _(i):
        def unit(lag):
            return lax.rem(i - lag + 1, nz)

        if nc > 1:

            @pl.when(i < nz)
            def _():
                stage_0(unit(0))

        @pl.when((i >= 1) & (i < nz + 1))
        def _():
            stage_1(unit(1))

        @pl.when(i < nz)
        def _():
            on_a_y(i)

        for d in range(1, nz):

            @pl.when(i == d)
            def _():
                far_z(d, on_b)

        @pl.when((i >= 1) & (i < nz + 1))
        def _():
            on_a_x(i - 1)

        @pl.when((i >= 2) & (i < nz + 2))
        def _():
            stage_2(unit(2))

        @pl.when((i >= 3) & (i < nz + 2))
        def _():
            stage_3_send(unit(3))

        @pl.when(i == nz)
        def _():
            rotate_half()

        @pl.when(i == nz + 1)
        def _():
            rotate()
            sent_bases()

    row = lax.broadcasted_iota(jnp.int32, (slab, width), 0) + (me.z * ny + me.y) * slab
    column = lax.broadcasted_iota(jnp.int32, (slab, width), 1)
    for j in range(per_owner):
        value = stage_3(0, j)
        for d in range(1, nz):
            copy_3(j, d).wait_recv()
            value = value + got_3[d, j].astype(f32)
        order = order_of(first + j, sector_slot, orders, sectors)
        inside = jnp.maximum(row, column) < order
        out[j] = jnp.where(inside, value, 0.0).astype(out.dtype)

    for p in range(count):
        give_rotated(p).wait()
    for j in odd:
        for f in range(nx):
            sent_z(b_z(j, f), lambda z: base_strip(j, z, f))
    if nc > 1:
        for j in range(per_owner):
            for f in range(nx):

                @pl.loop(0, nz)
                def _(z):
                    core(j, f, z).wait_send()

    @pl.loop(0, nz)
    def _(d):
        for j in range(per_owner):
            if nc > 1:
                for x in range(nx):
                    core_copy(x, j, d).wait_send()
            for k in range(1, size[axes(j)[0]]):
                copy_1(j, d, k).wait_send()
            for h in range(1, size[axes(j)[1]]):
                copy_2(j, d, h).wait_send()

    @pl.loop(1, nz)
    def _(d):
        for j in range(per_owner):
            copy_3(j, d).wait_send()


def sigma_and_rotation(
    dims, wavefunction, sector_bases, left, right, source, target, sector_slot, orders
):
    nx, nc, nz, ny = dims
    per_owner, slab, width = wavefunction.shape
    sectors = sector_slot.shape[0]
    most = max(nx, ny)
    dma = pltpu.SemaphoreType.DMA
    bf16, f32 = jnp.bfloat16, jnp.float32
    full = (per_owner, nz * ny * slab, width)
    return pl.pallas_call(
        functools.partial(sigma_kernel, dims, sectors),
        out_shape=(
            jax.ShapeDtypeStruct((per_owner, slab, width), bf16),
            jax.ShapeDtypeStruct(left.shape, bf16),
        ),
        in_specs=[VMEM, VMEM, ANY, ANY, SMEM, SMEM, SMEM, SMEM],
        out_specs=(VMEM, ANY),
        scratch_shapes=[
            pltpu.VMEM(full, bf16),
            pltpu.VMEM((sectors, nz * ny * slab, width), bf16),
            pltpu.VMEM(full, bf16),
            pltpu.VMEM(full, bf16),
            pltpu.VMEM(left.shape, bf16),
            pltpu.VMEM(left.shape, bf16),
            pltpu.VMEM(right.shape, bf16),
            pltpu.VMEM(left.shape, f32),
            pltpu.VMEM((nz, per_owner, nx, ny * slab, width), bf16),
            pltpu.VMEM((nz, per_owner, nx, ny * slab, width), bf16),
            pltpu.VMEM((nz, per_owner, most, most, slab, width), bf16),
            pltpu.VMEM((nz, per_owner, most, most, slab, width), bf16),
            pltpu.VMEM((nz, per_owner, most, slab, width), f32),
            pltpu.VMEM((nz, per_owner, most, slab, width), bf16),
            pltpu.VMEM((nz, per_owner, most, slab, width), bf16),
            pltpu.VMEM((nz, per_owner, slab, width), f32),
            pltpu.VMEM((nz, per_owner, slab, width), bf16),
            pltpu.VMEM((nz, per_owner, slab, width), bf16),
        ]
        + [dma((5,)), dma((left.shape[0],))]
        + [dma((2, nz)), dma((nz,))]
        + [dma((ny, nz))] * 2
        + [dma((2, per_owner, nz)), dma((per_owner, nz))]
        + [dma((per_owner, ny, nz))] * 2
        + [dma((per_owner, nx, ny, nz))] * 2
        + [dma((per_owner, nx))] * 2
        + [dma((per_owner, nx, ny))] * 2
        + [dma((2, per_owner, nx, nz)), dma((per_owner, nx, nz))]
        + [dma((per_owner, nx, nz))] * 2
        + [dma((nz, per_owner, nx))] * 2
        + [dma((nz, per_owner, most))] * 4
        + [dma((nz, per_owner))] * 2,
        compiler_params=pltpu.CompilerParams(
            collective_id=0, has_side_effects=True, vmem_limit_bytes=60 * 1024 * 1024
        ),
        name="sigma",
    )(wavefunction, sector_bases, left, right, source, target, sector_slot, orders)


def solution(mesh):
    dims = grid_of(mesh.shape["sector"], mesh.shape["op"])

    def per_device(
        wavefunction, sector_bases, left_env, right_env, pair_source, pair_target, sector_slot, orders
    ):
        return sigma_and_rotation(
            dims, wavefunction, sector_bases, left_env, right_env,
            pair_source, pair_target, sector_slot, orders,
        )

    placed = (
        P("sector", "op", None),
        P("sector", "op", None),
        P(("sector", "op"), None, None),
        P(("sector", "op"), None, None),
        P(("sector", "op")),
        P(("sector", "op")),
        P(),
        P(),
    )
    return jax.shard_map(
        per_device,
        mesh=mesh,
        in_specs=placed,
        out_specs=(P("sector", "op", None), P(("sector", "op"), None, None)),
        check_vma=False,
    )
```

```python
import functools

import jax
import jax.numpy as jnp
from jax import lax
from jax.experimental import pallas as pl
from jax.experimental.pallas import tpu as pltpu
from jax.sharding import PartitionSpec as P

MESH = pl.DeviceIdType.MESH
ANY = pl.BlockSpec(memory_space=pl.ANY)
VMEM = pl.BlockSpec(memory_space=pltpu.VMEM)
SMEM = pl.BlockSpec(memory_space=pltpu.SMEM)


def grid_of(n_sector, n_op):
    cores = 2 if n_sector % 2 == 0 else 1
    ny = 1
    while ny * ny * 4 <= n_op and n_op % (ny * 2) == 0:
        ny *= 2
    return n_sector // cores, cores, n_op // ny, ny


class Place:
    def __init__(self, dims):
        self.dims = dims
        nx, nc, nz, ny = dims
        sector, op = lax.axis_index("sector"), lax.axis_index("op")
        self.x, self.c = sector // nc, sector % nc
        self.z, self.y = op // ny, op % ny

    def at(self, x=0, c=0, z=0, y=0):
        nx, nc, nz, ny = self.dims
        return (
            lax.rem(self.x + x, nx),
            lax.rem(self.c + c, nc),
            lax.rem(self.z + z, nz),
            lax.rem(self.y + y, ny),
        )

    def device(self, **shift):
        nx, nc, nz, ny = self.dims
        x, c, z, y = self.at(**shift)
        return (x * nc + c, z * ny + y)

    def greet(self):
        barrier = pltpu.get_barrier_semaphore()
        count = 0
        for name, n in zip("xczy", self.dims):
            for shift in range(1, n):
                pl.semaphore_signal(
                    barrier, inc=1, device_id=self.device(**{name: shift}), device_id_type=MESH
                )
                count += 1
        pl.semaphore_wait(barrier, count)


def remote(src, dst, send, recv, device):
    return pltpu.make_async_remote_copy(
        src_ref=src, dst_ref=dst, send_sem=send, recv_sem=recv, device_id=device, device_id_type=MESH
    )


def order_of(slot, sector_slot, orders, sectors):
    total = jnp.int32(0)
    for i in range(sectors):
        total = total + jnp.where(sector_slot[i] == slot, orders[i], 0)
    return total


PLAN = {
    "wave": (-27.1, 2.7, 0.0),
    "a": (-21.8, 7.6, 0.0),
    "a_y": (-2.8, 4.8, 0.0),
    "a_x": (13.0, 3.8, 0.0),
    "b": (0.3, 6.6, 9.2),
    "start_b_x": (-31.0, 0.0, 0.0),
    "start_b_z": (-1.1, 0.0, -2.8),
    "start_a_z": (-23.7, 0.0, 0.0),
    "start_a_y": (-24.5, 0.0, 0.0),
    "pair": (0.1, 0.6, 0.0),
    "stage_0": (6.3, 1.7, 0.0),
    "stage_1": (9.7, 3.1, 0.0),
    "stage_2": (13.7, 5.0, 0.0),
    "stage_3": (19.0, 9.4, 0.0),
    "half": (39.8, 0.0, 0.0),
    "rotate": (55.1, 0.0, 0.0),
}


def timed(name, d=0, f=0):
    start, step, inner = PLAN[name]
    return start + step * d + inner * f


def sigma_kernel(
    dims, sectors, wave_ref, base_ref, left_hbm, right_hbm, source, target, sector_slot, orders,
    out, rotated_hbm,
    wave_all, base_all, masked, own_bases, half, left, right, product,
    send_c, got_c, send_1, got_1, mid, send_2, got_2, held, send_3, got_3,
    local, give, wzs, wzr, wys, wyr, azs, azr, ays, ayr, axs, axr,
    bys, byr, bxs, bxr, bzs, bzr, kcs, kcr,
    cs, cr, s1, r1, s2, r2, s3, r3,
):
    nx, nc, nz, ny = dims
    me = Place(dims)
    per_owner, slab, width = out.shape
    count = left.shape[0]
    strip = ny * slab
    f32, bf16 = jnp.float32, jnp.bfloat16
    size = {"x": nx, "y": ny}
    first = (me.x * nc + me.c) * per_owner
    even = list(range(0, per_owner, 2))
    odd = list(range(1, per_owner, 2))

    def rows(z, y):
        return pl.ds((z * ny + y) * slab, slab)

    def wave(j, z, e=0):
        return wave_all.at[j, rows(z, lax.rem(me.y + ny - e, ny)), :]

    def slot_of(j, f, g=0):
        x, c, _, _ = me.at(x=nx - f, c=nc - g)
        return (x * nc + c) * per_owner + j

    def base(j, z, e=0, f=0):
        return base_all.at[slot_of(j, f), rows(z, lax.rem(me.y + ny - e, ny)), :]

    def base_strip(j, z, f, g=0):
        return base_all.at[slot_of(j, f, g), pl.ds(z * strip, strip), :]

    keep_wave = pltpu.make_async_copy(
        wave_ref, wave_all.at[:, rows(me.z, me.y), :], local.at[0]
    )
    keep_base = pltpu.make_async_copy(
        base_ref, base_all.at[pl.ds(first, per_owner), rows(me.z, me.y), :], local.at[1]
    )
    take_left = pltpu.make_async_copy(left_hbm, left, local.at[2])
    take_right = pltpu.make_async_copy(right_hbm, right, local.at[3])

    def chain(src, dst, send, recv, up):
        return remote(src, dst, send, recv, me.device(z=1 if up else nz - 1))

    def wave_z(j):
        def copy(up, z, src):
            return chain(src, wave(j, z), wzs.at[0 if up else 1, j, z], wzr.at[j, z], up)

        return copy

    def wave_y(j, z, e, src):
        return remote(src, wave(j, z), wys.at[j, e, z], wyr.at[j, e, z], me.device(y=e))

    def a_z(j):
        def copy(up, z, src):
            return chain(src, base(j, z), azs.at[0 if up else 1, j, z], azr.at[j, z], up)

        return copy

    def a_y(j, z, e, src):
        return remote(src, base(j, z), ays.at[j, e, z], ayr.at[j, e, z], me.device(y=e))

    def a_x(j, z, e, f, src):
        return remote(src, base(j, z, e), axs.at[j, f, e, z], axr.at[j, f, e, z], me.device(x=f))

    def b_y(j, e, src):
        return remote(src, base(j, me.z), bys.at[j, e], byr.at[j, e], me.device(y=e))

    def b_x(j, e, f, src):
        return remote(src, base(j, me.z, e), bxs.at[j, e, f], bxr.at[j, e, f], me.device(x=f))

    def b_z(j, f):
        def copy(up, z, src):
            return chain(
                src, base_strip(j, z, f), bzs.at[0 if up else 1, j, f, z], bzr.at[j, f, z], up
            )

        return copy

    def core(j, f, z):
        block = base_strip(j, z, f)
        return remote(block, block, kcs.at[j, f, z], kcr.at[j, f, z], me.device(c=1))

    def give_core(j, f, z):
        if nc > 1:
            core(j, f, z).start()

    def far_z(d, visit):
        @pl.when(me.z >= d)
        def _():
            visit(me.z - d, True)

        @pl.when(me.z + d < nz)
        def _():
            visit(me.z + d, False)

    def both_ways(start, src):
        @pl.when(me.z < nz - 1)
        def _():
            start(True, me.z, src).start()

        @pl.when(me.z > 0)
        def _():
            start(False, me.z, src).start()

    def relay(copy, block, z, up):
        copy(up, z, block).wait_recv()

        @pl.when(me.z < nz - 1 if up else me.z > 0)
        def _():
            copy(up, z, block).start()

    def sent_z(start, block):
        @pl.when(me.z < nz - 1)
        def _():
            @pl.loop(0, me.z + 1)
            def _(z):
                start(True, z, block(z)).wait_send()

        @pl.when(me.z > 0)
        def _():
            @pl.loop(me.z, nz)
            def _(z):
                start(False, z, block(z)).wait_send()

    def on_wave(z, up):
        for j in range(per_owner):
            block = wave(j, z)
            relay(wave_z(j), block, z, up)
            for e in range(1, ny):
                wave_y(j, z, e, block).start()

    def on_b_y():
        keep_base.wait()
        for j in odd:
            for e in range(1, ny):
                b_y(j, e, base(j, me.z, e)).wait_recv()
                for f in range(1, nx):
                    b_x(j, e, f, base(j, me.z, e)).start()

    me.greet()
    for j in odd:
        for e in range(1, ny):
            b_y(j, e, base_ref.at[j]).start()
    for j in range(per_owner):
        both_ways(wave_z(j), wave_ref.at[j])
        for e in range(1, ny):
            wave_y(j, me.z, e, wave_ref.at[j]).start()
    for f in range(1, nx):
        for j in odd:
            b_x(j, 0, f, base_ref.at[j]).start()
        for j in even:
            a_x(j, me.z, 0, f, base_ref.at[j]).start()
    keep_wave.start()
    keep_base.start()
    take_left.start()
    take_right.start()
    def a_start_z():
        for j in even:
            both_ways(a_z(j), base_ref.at[j])

    def a_start_y():
        for j in even:
            for e in range(1, ny):
                a_y(j, me.z, e, base_ref.at[j]).start()

    def on_a(z, up):
        for j in even:
            block = base(j, z)
            relay(a_z(j), block, z, up)
            for e in range(1, ny):
                a_y(j, z, e, block).start()
            for f in range(1, nx):
                a_x(j, z, 0, f, block).start()

    def on_b_x(f):
        for j in odd:
            if f:
                for e in range(ny):
                    b_x(j, e, f, base(j, me.z, e, f)).wait_recv()
            block = base_strip(j, me.z, f)
            both_ways(b_z(j, f), block)
            give_core(j, f, me.z)

    def on_b(f, z, up):
        for j in odd:
            block = base_strip(j, z, f)
            relay(b_z(j, f), block, z, up)
            give_core(j, f, z)

    def on_a_y(z, up=True):
        for j in even:
            for e in range(1, ny):
                block = base(j, z, e)
                a_y(j, z, e, block).wait_recv()
                for f in range(1, nx):
                    a_x(j, z, e, f, block).start()
            give_core(j, 0, z)

    def on_a_x(z, up=True):
        for j in even:
            for f in range(1, nx):
                for e in range(ny):
                    a_x(j, z, e, f, base(j, z, e, f)).wait_recv()
                give_core(j, f, z)

    def take_wave():
        keep_wave.wait()
        take_left.wait()
        take_right.wait()
        for e in range(1, ny):

            @pl.loop(0, nz)
            def _(z):
                for j in range(per_owner):
                    wave_y(j, z, e, wave(j, z, e)).wait_recv()

        row = lax.broadcasted_iota(jnp.int32, (width, width), 0)
        column = lax.broadcasted_iota(jnp.int32, (width, width), 1)
        for j in range(per_owner):
            order = order_of(first + j, sector_slot, orders, sectors)
            inside = jnp.maximum(row, column) < order
            masked[j] = jnp.where(inside, wave_all[j], jnp.zeros((), bf16))

    def multiply(p):
        a = lax.rem(sector_slot[source[p]], per_owner)
        projected = jnp.dot(left[p], masked[a], preferred_element_type=f32)
        product[p] = lax.dot_general(
            projected.astype(bf16), right[p], (((1,), (1,)), ((), ())),
            preferred_element_type=f32,
        )

    landed = [sector_slot[target[p]] for p in range(count)]

    def partial_sum(slot, start, size):
        total = None
        for p in range(count):
            weight = jnp.where(landed[p] == slot, 1.0, 0.0).astype(f32)
            term = product[p, pl.ds(start, size), :] * weight
            total = term if total is None else total + term
        return total

    def axes(j):
        return ("x", "y") if j % 2 == 0 else ("y", "x")

    def zq(d):
        return lax.rem(me.z + d, nz)

    def core_copy(x, j, d):
        return remote(
            send_c.at[d, j, x], got_c.at[d, j, x], cs.at[d, j, x], cr.at[d, j, x], me.device(c=1)
        )

    def copy_1(j, d, k):
        return remote(
            send_1.at[d, j, k], got_1.at[d, j, k], s1.at[d, j, k], r1.at[d, j, k],
            me.device(**{axes(j)[0]: k}),
        )

    def copy_2(j, d, k):
        return remote(
            send_2.at[d, j, k], got_2.at[d, j, k], s2.at[d, j, k], r2.at[d, j, k],
            me.device(**{axes(j)[1]: k}),
        )

    def copy_3(j, d):
        return remote(
            send_3.at[d, j], got_3.at[d, j], s3.at[d, j], r3.at[d, j], me.device(z=d)
        )

    def stage_0(d):
        @pl.loop(0, per_owner * nx)
        def _(i):
            j, x = i // nx, lax.rem(i, nx)
            slot = (x * nc + lax.rem(me.c + 1, nc)) * per_owner + j
            for m in range(ny):
                value = partial_sum(slot, pl.multiple_of(zq(d) * strip + m * slab, slab), slab)
                send_c[d, j, x, pl.ds(m * slab, slab), :] = value.astype(bf16)
            core_copy(x, j, d).start()

    def stage_1(d):
        for j in range(per_owner):
            n1 = size[axes(j)[0]]
            n2 = size[axes(j)[1]]
            if nc > 1:
                for x in range(nx):
                    core_copy(x, j, d).wait_recv()
            for k in list(range(1, n1)) + [0]:

                @pl.loop(0, n2)
                def _(m):
                    if axes(j)[0] == "x":
                        x, y = lax.rem(me.x + k, nx), m
                    else:
                        x, y = m, lax.rem(me.y + k, ny)
                    offset = pl.multiple_of(y * slab, slab)
                    slot = (x * nc + me.c) * per_owner + j
                    value = partial_sum(slot, pl.multiple_of(zq(d) * strip + offset, slab), slab)
                    if nc > 1:
                        value = value + got_c[d, j, x, pl.ds(offset, slab), :].astype(f32)
                    if k:
                        send_1[d, j, k, m] = value.astype(bf16)
                    else:
                        mid[d, j, m] = value
                if k:
                    copy_1(j, d, k).start()

    def stage_2(d):
        for j in range(per_owner):
            axis_1, axis_2 = axes(j)
            n1, n2 = size[axis_1], size[axis_2]
            for k in range(1, n1):
                copy_1(j, d, k).wait_recv()
            for h in list(range(1, n2)) + [0]:
                m = lax.rem(getattr(me, axis_2) + h, n2)
                value = mid[d, j, m]
                for k in range(1, n1):
                    value = value + got_1[d, j, k, m].astype(f32)
                if h:
                    send_2[d, j, h] = value.astype(bf16)
                    copy_2(j, d, h).start()
                else:
                    held[d, j] = value

    def stage_3(d, j):
        for h in range(1, size[axes(j)[1]]):
            copy_2(j, d, h).wait_recv()
        value = held[d, j]
        for h in range(1, size[axes(j)[1]]):
            value = value + got_2[d, j, h].astype(f32)
        return value

    def stage_3_send(d):
        for j in range(per_owner):
            send_3[d, j] = stage_3(d, j).astype(bf16)
            copy_3(j, d).start()

    take_bases = pltpu.make_async_copy(
        base_all.at[pl.ds(first, per_owner)], own_bases, local.at[4]
    )

    def rotate_half():
        take_bases.start()
        take_bases.wait()
        for p in range(count):
            a = lax.rem(sector_slot[source[p]], per_owner)
            half[p] = jnp.dot(left[p], own_bases[a], preferred_element_type=f32).astype(bf16)

    def give_rotated(p):
        return pltpu.make_async_copy(right.at[p], rotated_hbm.at[p], give.at[p])

    def rotate():
        if nc > 1:
            for j in range(per_owner):
                for f in range(nx):

                    @pl.loop(0, nz)
                    def _(z):
                        core(j, f, z).wait_recv()

        for p in range(count):
            right[p] = lax.dot_general(
                base_all[sector_slot[target[p]]], half[p], (((0,), (0,)), ((), ())),
                preferred_element_type=f32,
            ).astype(bf16)
            give_rotated(p).start()

    def sent_bases():
        for j in range(per_owner):
            sent_z(wave_z(j), functools.partial(wave, j))

        @pl.loop(0, nz)
        def _(z):
            for j in range(per_owner):
                for e in range(1, ny):
                    wave_y(j, z, e, wave(j, z)).wait_send()
            for j in even:
                for e in range(1, ny):
                    a_y(j, z, e, base(j, z)).wait_send()
                for f in range(1, nx):
                    for e in range(ny):
                        a_x(j, z, e, f, base(j, z, e)).wait_send()

        for j in even:
            sent_z(a_z(j), functools.partial(base, j))
        for j in odd:
            for e in range(1, ny):
                b_y(j, e, base(j, me.z)).wait_send()
            for f in range(1, nx):
                for e in range(ny):
                    b_x(j, e, f, base(j, me.z, e)).wait_send()

    tasks = []

    def plan(key, visit, *args):
        tasks.append((key, len(tasks), visit, args))

    def after(key, *names):
        return max([key] + [done[name] for name in names])

    def step(name, d, f, needs, visit, *args):
        done[name, d, f] = after(timed(name, d, f), *needs)
        plan(done[name, d, f], visit, *args)

    done = {}
    for d in range(1, nz):
        plan(min(timed("wave", d), 0.0), far_z, d, on_wave)
    step("start_b_x", 0, 0, [], on_b_y)
    step("start_a_z", 0, 0, [], a_start_z)
    step("start_a_y", 0, 0, [("start_b_x", 0, 0)], a_start_y)
    for f in range(nx):
        step("start_b_z", 0, f, [("start_b_x", 0, 0)], on_b_x, f)
    for d in range(nz):
        before = ("a", d - 1, 0) if d > 1 else ("start_a_z", 0, 0)
        if d:
            step("a", d, 0, [before], far_z, d, on_a)
        for name, needs, visit in (
            ("a_y", ("a", d, 0) if d else ("start_a_y", 0, 0), on_a_y),
            ("a_x", ("a_y", d, 0), on_a_x),
        ):
            if d:
                step(name, d, 0, [needs], far_z, d, visit)
            else:
                step(name, d, 0, [needs], visit, me.z)
    for d in range(1, nz):
        for f in range(nx):
            before = ("b", d - 1, f) if d > 1 else ("start_b_z", 0, f)
            step("b", d, f, [before], far_z, d, functools.partial(on_b, f))
    bases = [name for name in done]
    plan(0.0, take_wave)
    for p in range(count):
        step("pair", p, 0, [], multiply, p)
    for u in range(nz):
        d = (u + 1) % nz
        needs = [("pair", count - 1, 0)]
        for name, visit in (
            ("stage_0", stage_0 if nc > 1 else None), ("stage_1", stage_1),
            ("stage_2", stage_2), ("stage_3", stage_3_send if d else None),
        ):
            if visit:
                step(name, u, 0, needs + ([(name, u - 1, 0)] if u else []), visit, d)
                needs = [(name, u, 0)]
    step("half", 0, 0, bases, rotate_half)
    step("rotate", 0, 0, [("half", 0, 0)], rotate)
    for _, _, visit, args in sorted(tasks, key=lambda task: task[:2]):
        visit(*args)
    sent_bases()
    for j in odd:
        for f in range(nx):
            sent_z(b_z(j, f), lambda z: base_strip(j, z, f))
    if nc > 1:
        for j in range(per_owner):
            for f in range(nx):

                @pl.loop(0, nz)
                def _(z):
                    core(j, f, z).wait_send()

    @pl.loop(0, nz)
    def _(d):
        for j in range(per_owner):
            if nc > 1:
                for x in range(nx):
                    core_copy(x, j, d).wait_send()
            for k in range(1, size[axes(j)[0]]):
                copy_1(j, d, k).wait_send()
            for h in range(1, size[axes(j)[1]]):
                copy_2(j, d, h).wait_send()

    row = lax.broadcasted_iota(jnp.int32, (slab, width), 0) + (me.z * ny + me.y) * slab
    column = lax.broadcasted_iota(jnp.int32, (slab, width), 1)
    for j in range(per_owner):
        value = stage_3(0, j)
        for d in range(1, nz):
            copy_3(j, d).wait_recv()
            value = value + got_3[d, j].astype(f32)
        order = order_of(first + j, sector_slot, orders, sectors)
        inside = jnp.maximum(row, column) < order
        out[j] = jnp.where(inside, value, 0.0).astype(out.dtype)

    for p in range(count):
        give_rotated(p).wait()
    @pl.loop(1, nz)
    def _(d):
        for j in range(per_owner):
            copy_3(j, d).wait_send()


def sigma_and_rotation(
    dims, wavefunction, sector_bases, left, right, source, target, sector_slot, orders
):
    nx, nc, nz, ny = dims
    per_owner, slab, width = wavefunction.shape
    sectors = sector_slot.shape[0]
    most = max(nx, ny)
    dma = pltpu.SemaphoreType.DMA
    bf16, f32 = jnp.bfloat16, jnp.float32
    full = (per_owner, nz * ny * slab, width)
    return pl.pallas_call(
        functools.partial(sigma_kernel, dims, sectors),
        out_shape=(
            jax.ShapeDtypeStruct((per_owner, slab, width), bf16),
            jax.ShapeDtypeStruct(left.shape, bf16),
        ),
        in_specs=[VMEM, VMEM, ANY, ANY, SMEM, SMEM, SMEM, SMEM],
        out_specs=(VMEM, ANY),
        scratch_shapes=[
            pltpu.VMEM(full, bf16),
            pltpu.VMEM((sectors, nz * ny * slab, width), bf16),
            pltpu.VMEM(full, bf16),
            pltpu.VMEM(full, bf16),
            pltpu.VMEM(left.shape, bf16),
            pltpu.VMEM(left.shape, bf16),
            pltpu.VMEM(right.shape, bf16),
            pltpu.VMEM(left.shape, f32),
            pltpu.VMEM((nz, per_owner, nx, ny * slab, width), bf16),
            pltpu.VMEM((nz, per_owner, nx, ny * slab, width), bf16),
            pltpu.VMEM((nz, per_owner, most, most, slab, width), bf16),
            pltpu.VMEM((nz, per_owner, most, most, slab, width), bf16),
            pltpu.VMEM((nz, per_owner, most, slab, width), f32),
            pltpu.VMEM((nz, per_owner, most, slab, width), bf16),
            pltpu.VMEM((nz, per_owner, most, slab, width), bf16),
            pltpu.VMEM((nz, per_owner, slab, width), f32),
            pltpu.VMEM((nz, per_owner, slab, width), bf16),
            pltpu.VMEM((nz, per_owner, slab, width), bf16),
        ]
        + [dma((5,)), dma((left.shape[0],))]
        + [dma((2, per_owner, nz)), dma((per_owner, nz))]
        + [dma((per_owner, ny, nz))] * 2
        + [dma((2, per_owner, nz)), dma((per_owner, nz))]
        + [dma((per_owner, ny, nz))] * 2
        + [dma((per_owner, nx, ny, nz))] * 2
        + [dma((per_owner, ny))] * 2
        + [dma((per_owner, ny, nx))] * 2
        + [dma((2, per_owner, nx, nz)), dma((per_owner, nx, nz))]
        + [dma((per_owner, nx, nz))] * 2
        + [dma((nz, per_owner, nx))] * 2
        + [dma((nz, per_owner, most))] * 4
        + [dma((nz, per_owner))] * 2,
        compiler_params=pltpu.CompilerParams(
            collective_id=0, has_side_effects=True, vmem_limit_bytes=60 * 1024 * 1024
        ),
        name="sigma",
    )(wavefunction, sector_bases, left, right, source, target, sector_slot, orders)


def hand_over_kernel(sigma, rotated, sigma_out, rotated_out, sigma_held, held, into, back):
    count = rotated.shape[0]

    def take(p):
        return pltpu.make_async_copy(rotated.at[p], held.at[p], into.at[p])

    def give(p):
        return pltpu.make_async_copy(held.at[p], rotated_out.at[p], back.at[p])

    take_sigma = pltpu.make_async_copy(sigma, sigma_held, into.at[count])
    give_sigma = pltpu.make_async_copy(sigma_held, sigma_out, back.at[count])
    for p in range(count):
        take(p).start()
    take_sigma.start()
    for p in range(count):
        take(p).wait()
        give(p).start()
    take_sigma.wait()
    give_sigma.start()
    for p in range(count):
        give(p).wait()
    give_sigma.wait()


def hand_over(sigma, rotated):
    count = rotated.shape[0]
    dma = pltpu.SemaphoreType.DMA
    return pl.pallas_call(
        hand_over_kernel,
        out_shape=(
            jax.ShapeDtypeStruct(sigma.shape, sigma.dtype),
            jax.ShapeDtypeStruct(rotated.shape, rotated.dtype),
        ),
        in_specs=[ANY, ANY],
        out_specs=(ANY, ANY),
        scratch_shapes=[
            pltpu.VMEM(sigma.shape, sigma.dtype),
            pltpu.VMEM(rotated.shape, rotated.dtype),
            dma((count + 1,)),
            dma((count + 1,)),
        ],
        compiler_params=pltpu.CompilerParams(vmem_limit_bytes=60 * 1024 * 1024),
        name="hand_over",
    )(sigma, rotated)


def solution(mesh):
    dims = grid_of(mesh.shape["sector"], mesh.shape["op"])

    def per_device(
        wavefunction, sector_bases, left_env, right_env, pair_source, pair_target, sector_slot, orders
    ):
        return hand_over(
            *sigma_and_rotation(
                dims, wavefunction, sector_bases, left_env, right_env,
                pair_source, pair_target, sector_slot, orders,
            )
        )

    placed = (
        P("sector", "op", None),
        P("sector", "op", None),
        P(("sector", "op"), None, None),
        P(("sector", "op"), None, None),
        P(("sector", "op")),
        P(("sector", "op")),
        P(),
        P(),
    )
    return jax.shard_map(
        per_device,
        mesh=mesh,
        in_specs=placed,
        out_specs=(P("sector", "op", None), P(("sector", "op"), None, None)),
        check_vma=False,
    )
```

```python
import functools

import jax
import jax.numpy as jnp
from jax import lax
from jax.experimental import pallas as pl
from jax.experimental.pallas import tpu as pltpu
from jax.sharding import PartitionSpec as P

MESH = pl.DeviceIdType.MESH
ANY = pl.BlockSpec(memory_space=pl.ANY)
VMEM = pl.BlockSpec(memory_space=pltpu.VMEM)
SMEM = pl.BlockSpec(memory_space=pltpu.SMEM)


def grid_of(n_sector, n_op):
    cores = 2 if n_sector % 2 == 0 else 1
    ny = 1
    while ny * ny * 4 <= n_op and n_op % (ny * 2) == 0:
        ny *= 2
    return n_sector // cores, cores, n_op // ny, ny


class Place:
    def __init__(self, dims):
        self.dims = dims
        nx, nc, nz, ny = dims
        sector, op = lax.axis_index("sector"), lax.axis_index("op")
        self.x, self.c = sector // nc, sector % nc
        self.z, self.y = op // ny, op % ny

    def at(self, x=0, c=0, z=0, y=0):
        nx, nc, nz, ny = self.dims
        return (
            lax.rem(self.x + x, nx),
            lax.rem(self.c + c, nc),
            lax.rem(self.z + z, nz),
            lax.rem(self.y + y, ny),
        )

    def device(self, **shift):
        nx, nc, nz, ny = self.dims
        x, c, z, y = self.at(**shift)
        return (x * nc + c, z * ny + y)

    def greet(self):
        barrier = pltpu.get_barrier_semaphore()
        nx, nc, nz, ny = self.dims
        count = 0
        for name, n in (("x", nx), ("c", nc), ("y", ny)):
            for shift in range(1, n):
                pl.semaphore_signal(
                    barrier, inc=1, device_id=self.device(**{name: shift}), device_id_type=MESH
                )
                count += 1
        for there, shift in ((self.z < nz - 1, 1), (self.z > 0, nz - 1)):

            @pl.when(there)
            def _():
                pl.semaphore_signal(
                    barrier, inc=1, device_id=self.device(z=shift), device_id_type=MESH
                )

        count = count + (self.z < nz - 1).astype(jnp.int32) + (self.z > 0).astype(jnp.int32)
        pl.semaphore_wait(barrier, count)


def remote(src, dst, send, recv, device):
    return pltpu.make_async_remote_copy(
        src_ref=src, dst_ref=dst, send_sem=send, recv_sem=recv, device_id=device, device_id_type=MESH
    )


def order_of(slot, sector_slot, orders, sectors):
    total = jnp.int32(0)
    for i in range(sectors):
        total = total + jnp.where(sector_slot[i] == slot, orders[i], 0)
    return total


PLAN = {
    "wave": (-27.1, 2.7, 0.0),
    "a": (-21.8, 7.6, 0.0),
    "a_y": (-2.8, 4.8, 0.0),
    "a_x": (13.0, 3.8, 0.0),
    "b": (0.3, 6.6, 9.2),
    "start_b_x": (-31.0, 0.0, 0.0),
    "start_b_z": (-1.1, 0.0, -2.8),
    "start_a_z": (-23.7, 0.0, 0.0),
    "start_a_y": (-24.5, 0.0, 0.0),
    "pair": (0.1, 0.6, 0.0),
    "stage_0": (6.3, 1.7, 0.0),
    "stage_1": (9.7, 3.1, 0.0),
    "stage_2": (13.7, 5.0, 0.0),
    "stage_3": (19.0, 9.4, 0.0),
    "half": (39.8, 0.0, 0.0),
    "rotate": (55.1, 0.0, 0.0),
}


def timed(name, d=0, f=0):
    start, step, inner = PLAN[name]
    return start + step * d + inner * f


def sigma_kernel(
    dims, sectors, wave_ref, base_ref, left_hbm, right_hbm, source, target, sector_slot, orders,
    out, rotated_hbm,
    wave_all, base_all, masked, own_bases, half, left, right, product,
    send_c, got_c, send_1, got_1, mid, send_2, got_2, held, send_3, got_3,
    local, give, wzs, wzr, wys, wyr, azs, azr, ays, ayr, axs, axr,
    bys, byr, bxs, bxr, bzs, bzr, kcs, kcr,
    cs, cr, s1, r1, s2, r2, s3, r3,
):
    nx, nc, nz, ny = dims
    me = Place(dims)
    per_owner, slab, width = out.shape
    count = left.shape[0]
    strip = ny * slab
    f32, bf16 = jnp.float32, jnp.bfloat16
    size = {"x": nx, "y": ny}
    first = (me.x * nc + me.c) * per_owner
    even = list(range(0, per_owner, 2))
    odd = list(range(1, per_owner, 2))

    def rows(z, y):
        return pl.ds((z * ny + y) * slab, slab)

    def wave(j, z, e=0):
        return wave_all.at[j, rows(z, lax.rem(me.y + ny - e, ny)), :]

    def slot_of(j, f, g=0):
        x, c, _, _ = me.at(x=nx - f, c=nc - g)
        return (x * nc + c) * per_owner + j

    def base(j, z, e=0, f=0):
        return base_all.at[slot_of(j, f), rows(z, lax.rem(me.y + ny - e, ny)), :]

    def base_strip(j, z, f, g=0):
        return base_all.at[slot_of(j, f, g), pl.ds(z * strip, strip), :]

    keep_wave = pltpu.make_async_copy(
        wave_ref, wave_all.at[:, rows(me.z, me.y), :], local.at[0]
    )
    keep_base = pltpu.make_async_copy(
        base_ref, base_all.at[pl.ds(first, per_owner), rows(me.z, me.y), :], local.at[1]
    )
    take_left = pltpu.make_async_copy(left_hbm, left, local.at[2])
    take_right = pltpu.make_async_copy(right_hbm, right, local.at[3])

    def chain(src, dst, send, recv, up):
        return remote(src, dst, send, recv, me.device(z=1 if up else nz - 1))

    def wave_z(j):
        def copy(up, z, src):
            return chain(src, wave(j, z), wzs.at[0 if up else 1, j, z], wzr.at[j, z], up)

        return copy

    def wave_y(j, z, e, src):
        return remote(src, wave(j, z), wys.at[j, e, z], wyr.at[j, e, z], me.device(y=e))

    def a_z(j):
        def copy(up, z, src):
            return chain(src, base(j, z), azs.at[0 if up else 1, j, z], azr.at[j, z], up)

        return copy

    def a_y(j, z, e, src):
        return remote(src, base(j, z), ays.at[j, e, z], ayr.at[j, e, z], me.device(y=e))

    def a_x(j, z, e, f, src):
        return remote(src, base(j, z, e), axs.at[j, f, e, z], axr.at[j, f, e, z], me.device(x=f))

    def b_y(j, e, src):
        return remote(src, base(j, me.z), bys.at[j, e], byr.at[j, e], me.device(y=e))

    def b_x(j, e, f, src):
        return remote(src, base(j, me.z, e), bxs.at[j, e, f], bxr.at[j, e, f], me.device(x=f))

    def b_z(j, f):
        def copy(up, z, src):
            return chain(
                src, base_strip(j, z, f), bzs.at[0 if up else 1, j, f, z], bzr.at[j, f, z], up
            )

        return copy

    def core(j, f, z):
        block = base_strip(j, z, f)
        return remote(block, block, kcs.at[j, f, z], kcr.at[j, f, z], me.device(c=1))

    def give_core(j, f, z):
        if nc > 1:
            core(j, f, z).start()

    def far_z(d, visit):
        @pl.when(me.z >= d)
        def _():
            visit(me.z - d, True)

        @pl.when(me.z + d < nz)
        def _():
            visit(me.z + d, False)

    def both_ways(start, src):
        @pl.when(me.z < nz - 1)
        def _():
            start(True, me.z, src).start()

        @pl.when(me.z > 0)
        def _():
            start(False, me.z, src).start()

    def relay(copy, block, z, up):
        copy(up, z, block).wait_recv()

        @pl.when(me.z < nz - 1 if up else me.z > 0)
        def _():
            copy(up, z, block).start()

    def sent_z(start, block):
        @pl.when(me.z < nz - 1)
        def _():
            @pl.loop(0, me.z + 1)
            def _(z):
                start(True, z, block(z)).wait_send()

        @pl.when(me.z > 0)
        def _():
            @pl.loop(me.z, nz)
            def _(z):
                start(False, z, block(z)).wait_send()

    def on_wave(z, up):
        for j in range(per_owner):
            block = wave(j, z)
            relay(wave_z(j), block, z, up)
            for e in range(1, ny):
                wave_y(j, z, e, block).start()

    def on_b_y():
        keep_base.wait()
        for j in odd:
            for e in range(1, ny):
                b_y(j, e, base(j, me.z, e)).wait_recv()
                for f in range(1, nx):
                    b_x(j, e, f, base(j, me.z, e)).start()

    me.greet()
    for j in odd:
        for e in range(1, ny):
            b_y(j, e, base_ref.at[j]).start()
    for j in range(per_owner):
        both_ways(wave_z(j), wave_ref.at[j])
        for e in range(1, ny):
            wave_y(j, me.z, e, wave_ref.at[j]).start()
    for f in range(1, nx):
        for j in odd:
            b_x(j, 0, f, base_ref.at[j]).start()
        for j in even:
            a_x(j, me.z, 0, f, base_ref.at[j]).start()
    keep_wave.start()
    keep_base.start()
    take_left.start()
    take_right.start()
    def a_start_z():
        for j in even:
            both_ways(a_z(j), base_ref.at[j])

    def a_start_y():
        for j in even:
            for e in range(1, ny):
                a_y(j, me.z, e, base_ref.at[j]).start()

    def on_a(z, up):
        for j in even:
            block = base(j, z)
            relay(a_z(j), block, z, up)
            for e in range(1, ny):
                a_y(j, z, e, block).start()
            for f in range(1, nx):
                a_x(j, z, 0, f, block).start()

    def on_b_x(f):
        for j in odd:
            if f:
                for e in range(ny):
                    b_x(j, e, f, base(j, me.z, e, f)).wait_recv()
            block = base_strip(j, me.z, f)
            both_ways(b_z(j, f), block)
            give_core(j, f, me.z)

    def on_b(f, z, up):
        for j in odd:
            block = base_strip(j, z, f)
            relay(b_z(j, f), block, z, up)
            give_core(j, f, z)

    def on_a_y(z, up=True):
        for j in even:
            for e in range(1, ny):
                block = base(j, z, e)
                a_y(j, z, e, block).wait_recv()
                for f in range(1, nx):
                    a_x(j, z, e, f, block).start()
            give_core(j, 0, z)

    def on_a_x(z, up=True):
        for j in even:
            for f in range(1, nx):
                for e in range(ny):
                    a_x(j, z, e, f, base(j, z, e, f)).wait_recv()
                give_core(j, f, z)

    def take_wave():
        keep_wave.wait()
        take_left.wait()
        take_right.wait()
        for e in range(1, ny):

            @pl.loop(0, nz)
            def _(z):
                for j in range(per_owner):
                    wave_y(j, z, e, wave(j, z, e)).wait_recv()

        row = lax.broadcasted_iota(jnp.int32, (width, width), 0)
        column = lax.broadcasted_iota(jnp.int32, (width, width), 1)
        for j in range(per_owner):
            order = order_of(first + j, sector_slot, orders, sectors)
            inside = jnp.maximum(row, column) < order
            masked[j] = jnp.where(inside, wave_all[j], jnp.zeros((), bf16))

    def multiply(p):
        a = lax.rem(sector_slot[source[p]], per_owner)
        projected = jnp.dot(left[p], masked[a], preferred_element_type=f32)
        product[p] = lax.dot_general(
            projected.astype(bf16), right[p], (((1,), (1,)), ((), ())),
            preferred_element_type=f32,
        )

    landed = [sector_slot[target[p]] for p in range(count)]

    def partial_sum(slot, start, size):
        total = None
        for p in range(count):
            weight = jnp.where(landed[p] == slot, 1.0, 0.0).astype(f32)
            term = product[p, pl.ds(start, size), :] * weight
            total = term if total is None else total + term
        return total

    def axes(j):
        return ("x", "y") if j % 2 == 0 else ("y", "x")

    def zq(d):
        return lax.rem(me.z + d, nz)

    def core_copy(x, j, d):
        return remote(
            send_c.at[d, j, x], got_c.at[d, j, x], cs.at[d, j, x], cr.at[d, j, x], me.device(c=1)
        )

    def copy_1(j, d, k):
        return remote(
            send_1.at[d, j, k], got_1.at[d, j, k], s1.at[d, j, k], r1.at[d, j, k],
            me.device(**{axes(j)[0]: k}),
        )

    def copy_2(j, d, k):
        return remote(
            send_2.at[d, j, k], got_2.at[d, j, k], s2.at[d, j, k], r2.at[d, j, k],
            me.device(**{axes(j)[1]: k}),
        )

    def copy_3(j, d):
        return remote(
            send_3.at[d, j], got_3.at[d, j], s3.at[d, j], r3.at[d, j], me.device(z=d)
        )

    def stage_0(d):
        @pl.loop(0, per_owner * nx)
        def _(i):
            j, x = i // nx, lax.rem(i, nx)
            slot = (x * nc + lax.rem(me.c + 1, nc)) * per_owner + j
            for m in range(ny):
                value = partial_sum(slot, pl.multiple_of(zq(d) * strip + m * slab, slab), slab)
                send_c[d, j, x, pl.ds(m * slab, slab), :] = value.astype(bf16)
            core_copy(x, j, d).start()

    def stage_1(d):
        for j in range(per_owner):
            n1 = size[axes(j)[0]]
            n2 = size[axes(j)[1]]
            if nc > 1:
                for x in range(nx):
                    core_copy(x, j, d).wait_recv()
            for k in list(range(1, n1)) + [0]:

                @pl.loop(0, n2)
                def _(m):
                    if axes(j)[0] == "x":
                        x, y = lax.rem(me.x + k, nx), m
                    else:
                        x, y = m, lax.rem(me.y + k, ny)
                    offset = pl.multiple_of(y * slab, slab)
                    slot = (x * nc + me.c) * per_owner + j
                    value = partial_sum(slot, pl.multiple_of(zq(d) * strip + offset, slab), slab)
                    if nc > 1:
                        value = value + got_c[d, j, x, pl.ds(offset, slab), :].astype(f32)
                    if k:
                        send_1[d, j, k, m] = value.astype(bf16)
                    else:
                        mid[d, j, m] = value
                if k:
                    copy_1(j, d, k).start()

    def stage_2(d):
        for j in range(per_owner):
            axis_1, axis_2 = axes(j)
            n1, n2 = size[axis_1], size[axis_2]
            for k in range(1, n1):
                copy_1(j, d, k).wait_recv()
            for h in list(range(1, n2)) + [0]:
                m = lax.rem(getattr(me, axis_2) + h, n2)
                value = mid[d, j, m]
                for k in range(1, n1):
                    value = value + got_1[d, j, k, m].astype(f32)
                if h:
                    send_2[d, j, h] = value.astype(bf16)
                    copy_2(j, d, h).start()
                else:
                    held[d, j] = value

    def stage_3(d, j):
        for h in range(1, size[axes(j)[1]]):
            copy_2(j, d, h).wait_recv()
        value = held[d, j]
        for h in range(1, size[axes(j)[1]]):
            value = value + got_2[d, j, h].astype(f32)
        return value

    def stage_3_send(d):
        for j in range(per_owner):
            send_3[d, j] = stage_3(d, j).astype(bf16)
            copy_3(j, d).start()

    take_bases = pltpu.make_async_copy(
        base_all.at[pl.ds(first, per_owner)], own_bases, local.at[4]
    )

    def rotate_half():
        take_bases.start()
        take_bases.wait()
        for p in range(count):
            a = lax.rem(sector_slot[source[p]], per_owner)
            half[p] = jnp.dot(left[p], own_bases[a], preferred_element_type=f32).astype(bf16)

    def give_rotated(p):
        return pltpu.make_async_copy(right.at[p], rotated_hbm.at[p], give.at[p])

    def rotate():
        if nc > 1:
            for j in range(per_owner):
                for f in range(nx):

                    @pl.loop(0, nz)
                    def _(z):
                        core(j, f, z).wait_recv()

        for p in range(count):
            right[p] = lax.dot_general(
                base_all[sector_slot[target[p]]], half[p], (((0,), (0,)), ((), ())),
                preferred_element_type=f32,
            ).astype(bf16)
            give_rotated(p).start()

    def sent_bases():
        for j in range(per_owner):
            sent_z(wave_z(j), functools.partial(wave, j))

        @pl.loop(0, nz)
        def _(z):
            for j in range(per_owner):
                for e in range(1, ny):
                    wave_y(j, z, e, wave(j, z)).wait_send()
            for j in even:
                for e in range(1, ny):
                    a_y(j, z, e, base(j, z)).wait_send()
                for f in range(1, nx):
                    for e in range(ny):
                        a_x(j, z, e, f, base(j, z, e)).wait_send()

        for j in even:
            sent_z(a_z(j), functools.partial(base, j))
        for j in odd:
            for e in range(1, ny):
                b_y(j, e, base(j, me.z)).wait_send()
            for f in range(1, nx):
                for e in range(ny):
                    b_x(j, e, f, base(j, me.z, e)).wait_send()

    tasks = []

    def plan(key, visit, *args):
        tasks.append((key, len(tasks), visit, args))

    def after(key, *names):
        return max([key] + [done[name] for name in names])

    def step(name, d, f, needs, visit, *args):
        done[name, d, f] = after(timed(name, d, f), *needs)
        plan(done[name, d, f], visit, *args)

    done = {}
    for d in range(1, nz):
        plan(min(timed("wave", d), 0.0), far_z, d, on_wave)
    step("start_b_x", 0, 0, [], on_b_y)
    step("start_a_z", 0, 0, [], a_start_z)
    step("start_a_y", 0, 0, [("start_b_x", 0, 0)], a_start_y)
    for f in range(nx):
        step("start_b_z", 0, f, [("start_b_x", 0, 0)], on_b_x, f)
    for d in range(nz):
        before = ("a", d - 1, 0) if d > 1 else ("start_a_z", 0, 0)
        if d:
            step("a", d, 0, [before], far_z, d, on_a)
        for name, needs, visit in (
            ("a_y", ("a", d, 0) if d else ("start_a_y", 0, 0), on_a_y),
            ("a_x", ("a_y", d, 0), on_a_x),
        ):
            if d:
                step(name, d, 0, [needs], far_z, d, visit)
            else:
                step(name, d, 0, [needs], visit, me.z)
    for d in range(1, nz):
        for f in range(nx):
            before = ("b", d - 1, f) if d > 1 else ("start_b_z", 0, f)
            step("b", d, f, [before], far_z, d, functools.partial(on_b, f))
    bases = [name for name in done]
    plan(0.0, take_wave)
    for p in range(count):
        step("pair", p, 0, [], multiply, p)
    for u in range(nz):
        d = (u + 1) % nz
        needs = [("pair", count - 1, 0)]
        for name, visit in (
            ("stage_0", stage_0 if nc > 1 else None), ("stage_1", stage_1),
            ("stage_2", stage_2), ("stage_3", stage_3_send if d else None),
        ):
            if visit:
                step(name, u, 0, needs + ([(name, u - 1, 0)] if u else []), visit, d)
                needs = [(name, u, 0)]
    step("half", 0, 0, bases, rotate_half)
    step("rotate", 0, 0, [("half", 0, 0)], rotate)
    for _, _, visit, args in sorted(tasks, key=lambda task: task[:2]):
        visit(*args)
    sent_bases()
    for j in odd:
        for f in range(nx):
            sent_z(b_z(j, f), lambda z: base_strip(j, z, f))
    if nc > 1:
        for j in range(per_owner):
            for f in range(nx):

                @pl.loop(0, nz)
                def _(z):
                    core(j, f, z).wait_send()

    @pl.loop(0, nz)
    def _(d):
        for j in range(per_owner):
            if nc > 1:
                for x in range(nx):
                    core_copy(x, j, d).wait_send()
            for k in range(1, size[axes(j)[0]]):
                copy_1(j, d, k).wait_send()
            for h in range(1, size[axes(j)[1]]):
                copy_2(j, d, h).wait_send()

    row = lax.broadcasted_iota(jnp.int32, (slab, width), 0) + (me.z * ny + me.y) * slab
    column = lax.broadcasted_iota(jnp.int32, (slab, width), 1)
    for j in range(per_owner):
        value = stage_3(0, j)
        for d in range(1, nz):
            copy_3(j, d).wait_recv()
            value = value + got_3[d, j].astype(f32)
        order = order_of(first + j, sector_slot, orders, sectors)
        inside = jnp.maximum(row, column) < order
        out[j] = jnp.where(inside, value, 0.0).astype(out.dtype)

    for p in range(count):
        give_rotated(p).wait()
    @pl.loop(1, nz)
    def _(d):
        for j in range(per_owner):
            copy_3(j, d).wait_send()


def sigma_and_rotation(
    dims, wavefunction, sector_bases, left, right, source, target, sector_slot, orders
):
    nx, nc, nz, ny = dims
    per_owner, slab, width = wavefunction.shape
    sectors = sector_slot.shape[0]
    most = max(nx, ny)
    dma = pltpu.SemaphoreType.DMA
    bf16, f32 = jnp.bfloat16, jnp.float32
    full = (per_owner, nz * ny * slab, width)
    return pl.pallas_call(
        functools.partial(sigma_kernel, dims, sectors),
        out_shape=(
            jax.ShapeDtypeStruct((per_owner, slab, width), bf16),
            jax.ShapeDtypeStruct(left.shape, bf16),
        ),
        in_specs=[ANY, ANY, ANY, ANY, SMEM, SMEM, SMEM, SMEM],
        out_specs=(VMEM, ANY),
        scratch_shapes=[
            pltpu.VMEM(full, bf16),
            pltpu.VMEM((sectors, nz * ny * slab, width), bf16),
            pltpu.VMEM(full, bf16),
            pltpu.VMEM(full, bf16),
            pltpu.VMEM(left.shape, bf16),
            pltpu.VMEM(left.shape, bf16),
            pltpu.VMEM(right.shape, bf16),
            pltpu.VMEM(left.shape, f32),
            pltpu.VMEM((nz, per_owner, nx, ny * slab, width), bf16),
            pltpu.VMEM((nz, per_owner, nx, ny * slab, width), bf16),
            pltpu.VMEM((nz, per_owner, most, most, slab, width), bf16),
            pltpu.VMEM((nz, per_owner, most, most, slab, width), bf16),
            pltpu.VMEM((nz, per_owner, most, slab, width), f32),
            pltpu.VMEM((nz, per_owner, most, slab, width), bf16),
            pltpu.VMEM((nz, per_owner, most, slab, width), bf16),
            pltpu.VMEM((nz, per_owner, slab, width), f32),
            pltpu.VMEM((nz, per_owner, slab, width), bf16),
            pltpu.VMEM((nz, per_owner, slab, width), bf16),
        ]
        + [dma((5,)), dma((left.shape[0],))]
        + [dma((2, per_owner, nz)), dma((per_owner, nz))]
        + [dma((per_owner, ny, nz))] * 2
        + [dma((2, per_owner, nz)), dma((per_owner, nz))]
        + [dma((per_owner, ny, nz))] * 2
        + [dma((per_owner, nx, ny, nz))] * 2
        + [dma((per_owner, ny))] * 2
        + [dma((per_owner, ny, nx))] * 2
        + [dma((2, per_owner, nx, nz)), dma((per_owner, nx, nz))]
        + [dma((per_owner, nx, nz))] * 2
        + [dma((nz, per_owner, nx))] * 2
        + [dma((nz, per_owner, most))] * 4
        + [dma((nz, per_owner))] * 2,
        compiler_params=pltpu.CompilerParams(
            collective_id=0, has_side_effects=True, vmem_limit_bytes=60 * 1024 * 1024
        ),
        name="sigma",
    )(wavefunction, sector_bases, left, right, source, target, sector_slot, orders)


def hand_over_kernel(sigma, rotated, sigma_out, rotated_out, sigma_held, held, into, back):
    count = rotated.shape[0]

    def take(p):
        return pltpu.make_async_copy(rotated.at[p], held.at[p], into.at[p])

    def give(p):
        return pltpu.make_async_copy(held.at[p], rotated_out.at[p], back.at[p])

    take_sigma = pltpu.make_async_copy(sigma, sigma_held, into.at[count])
    give_sigma = pltpu.make_async_copy(sigma_held, sigma_out, back.at[count])
    for p in range(count):
        take(p).start()
    take_sigma.start()
    for p in range(count):
        take(p).wait()
        give(p).start()
    take_sigma.wait()
    give_sigma.start()
    for p in range(count):
        give(p).wait()
    give_sigma.wait()


def hand_over(sigma, rotated):
    count = rotated.shape[0]
    dma = pltpu.SemaphoreType.DMA
    return pl.pallas_call(
        hand_over_kernel,
        out_shape=(
            jax.ShapeDtypeStruct(sigma.shape, sigma.dtype),
            jax.ShapeDtypeStruct(rotated.shape, rotated.dtype),
        ),
        in_specs=[ANY, ANY],
        out_specs=(ANY, ANY),
        scratch_shapes=[
            pltpu.VMEM(sigma.shape, sigma.dtype),
            pltpu.VMEM(rotated.shape, rotated.dtype),
            dma((count + 1,)),
            dma((count + 1,)),
        ],
        compiler_params=pltpu.CompilerParams(vmem_limit_bytes=60 * 1024 * 1024),
        name="hand_over",
    )(sigma, rotated)


def solution(mesh):
    dims = grid_of(mesh.shape["sector"], mesh.shape["op"])

    def per_device(
        wavefunction, sector_bases, left_env, right_env, pair_source, pair_target, sector_slot, orders
    ):
        return hand_over(
            *sigma_and_rotation(
                dims, wavefunction, sector_bases, left_env, right_env,
                pair_source, pair_target, sector_slot, orders,
            )
        )

    placed = (
        P("sector", "op", None),
        P("sector", "op", None),
        P(("sector", "op"), None, None),
        P(("sector", "op"), None, None),
        P(("sector", "op")),
        P(("sector", "op")),
        P(),
        P(),
    )
    return jax.shard_map(
        per_device,
        mesh=mesh,
        in_specs=placed,
        out_specs=(P("sector", "op", None), P(("sector", "op"), None, None)),
        check_vma=False,
    )
```

```python
import functools

import jax
import jax.numpy as jnp
from jax import lax
from jax.experimental import pallas as pl
from jax.experimental.pallas import tpu as pltpu
from jax.sharding import PartitionSpec as P

MESH = pl.DeviceIdType.MESH
ANY = pl.BlockSpec(memory_space=pl.ANY)
VMEM = pl.BlockSpec(memory_space=pltpu.VMEM)
SMEM = pl.BlockSpec(memory_space=pltpu.SMEM)


def grid_of(n_sector, n_op):
    cores = 2 if n_sector % 2 == 0 else 1
    ny = 1
    while ny * ny * 4 <= n_op and n_op % (ny * 2) == 0:
        ny *= 2
    return n_sector // cores, cores, n_op // ny, ny


class Place:
    def __init__(self, dims):
        self.dims = dims
        nx, nc, nz, ny = dims
        sector, op = lax.axis_index("sector"), lax.axis_index("op")
        self.x, self.c = sector // nc, sector % nc
        self.z, self.y = op // ny, op % ny

    def at(self, x=0, c=0, z=0, y=0):
        nx, nc, nz, ny = self.dims
        return (
            lax.rem(self.x + x, nx),
            lax.rem(self.c + c, nc),
            lax.rem(self.z + z, nz),
            lax.rem(self.y + y, ny),
        )

    def device(self, **shift):
        nx, nc, nz, ny = self.dims
        x, c, z, y = self.at(**shift)
        return (x * nc + c, z * ny + y)

    def greet(self):
        barrier = pltpu.get_barrier_semaphore()
        nx, nc, nz, ny = self.dims
        count = 0
        for name, n in (("x", nx), ("c", nc), ("y", ny)):
            for shift in range(1, n):
                pl.semaphore_signal(
                    barrier, inc=1, device_id=self.device(**{name: shift}), device_id_type=MESH
                )
                count += 1
        for there, shift in ((self.z < nz - 1, 1), (self.z > 0, nz - 1)):

            @pl.when(there)
            def _():
                pl.semaphore_signal(
                    barrier, inc=1, device_id=self.device(z=shift), device_id_type=MESH
                )

        count = count + (self.z < nz - 1).astype(jnp.int32) + (self.z > 0).astype(jnp.int32)
        pl.semaphore_wait(barrier, count)


def remote(src, dst, send, recv, device):
    return pltpu.make_async_remote_copy(
        src_ref=src, dst_ref=dst, send_sem=send, recv_sem=recv, device_id=device, device_id_type=MESH
    )


def order_of(slot, sector_slot, orders, sectors):
    total = jnp.int32(0)
    for i in range(sectors):
        total = total + jnp.where(sector_slot[i] == slot, orders[i], 0)
    return total


PLAN = {
    "wave": ((-8, -8, -5, -4),),
    "a": ((-3, -3, -2, 1),),
    "a_y": ((27, 7, 11, 35),),
    "a_x": ((34, 25, 39, 44),),
    "b": ((22, 22, 30, 41), (15, 15, 28, 42)),
    "start_b_x": ((-6,),),
    "start_b_z": ((5,), (-1,)),
    "start_a_z": ((-7,),),
    "start_a_y": ((12,),),
    "pair": ((2, 3, 4, 6, 8, 9), (16, 17, 19, 20, 21, 24)),
    "stage_0": ((10, 13, 26, 33),),
    "stage_1": ((14, 18, 29, 37),),
    "stage_2": ((23, 31, 36, 45),),
    "stage_3": ((32, 38, 40, 47),),
    "half": ((43,),),
    "rotate": ((46,),),
}


def timed(name, d=0, f=0):
    row = PLAN[name][min(f, len(PLAN[name]) - 1)]
    beyond = max(d - len(row) + 1, 0)
    return float(row[min(d, len(row) - 1)] + beyond * (row[-1] - row[max(len(row) - 2, 0)]))


def sigma_kernel(
    dims, sectors, wave_ref, base_ref, left_hbm, right_hbm,
    source_hbm, target_hbm, sector_slot_hbm, orders_hbm,
    out, rotated_hbm,
    wave_all, base_all, masked, own_bases, half, left, right, product,
    send_c, got_c, send_1, got_1, mid, send_2, got_2, held, send_3, got_3,
    local, give, wzs, wzr, wys, wyr, azs, azr, ays, ayr, axs, axr,
    bys, byr, bxs, bxr, bzs, bzr, kcs, kcr,
    cs, cr, s1, r1, s2, r2, s3, r3,
    source, target, sector_slot, orders, indices,
):
    nx, nc, nz, ny = dims
    me = Place(dims)
    per_owner, slab, width = out.shape
    count = left.shape[0]
    strip = ny * slab
    f32, bf16 = jnp.float32, jnp.bfloat16
    size = {"x": nx, "y": ny}
    first = (me.x * nc + me.c) * per_owner
    parts = 2 if nz % 2 == 0 else 1
    deep = nz // parts
    even = list(range(0, per_owner, 2))
    odd = list(range(1, per_owner, 2))

    def rows(z, y):
        return pl.ds((z * ny + y) * slab, slab)

    def wave(j, z, e=0):
        return wave_all.at[j, rows(z, lax.rem(me.y + ny - e, ny)), :]

    def part_of(part):
        return lax.rem(me.z // deep + 1 + part, parts)

    def z_of(u):
        part, step = u // deep, u % deep
        step = step + part + 2 - parts
        return part_of(part) * deep + lax.rem(me.z + step, deep)

    def slot_of(j, f, g=0):
        x, c, _, _ = me.at(x=nx - f, c=nc - g)
        return (x * nc + c) * per_owner + j

    def base(j, z, e=0, f=0):
        return base_all.at[slot_of(j, f), rows(z, lax.rem(me.y + ny - e, ny)), :]

    def base_strip(j, z, f, g=0):
        return base_all.at[slot_of(j, f, g), pl.ds(z * strip, strip), :]

    keep_wave = pltpu.make_async_copy(
        wave_ref, wave_all.at[:, rows(me.z, me.y), :], local.at[0]
    )
    keep_base = pltpu.make_async_copy(
        base_ref, base_all.at[pl.ds(first, per_owner), rows(me.z, me.y), :], local.at[1]
    )
    take_left = pltpu.make_async_copy(left_hbm, left, local.at[2])
    take_indices = [
        pltpu.make_async_copy(there, here, indices.at[i])
        for i, (there, here) in enumerate(
            (
                (source_hbm, source), (target_hbm, target),
                (sector_slot_hbm, sector_slot), (orders_hbm, orders),
            )
        )
    ]
    take_right = pltpu.make_async_copy(right_hbm, right, local.at[3])

    def chain(src, dst, send, recv, up):
        return remote(src, dst, send, recv, me.device(z=1 if up else nz - 1))

    def wave_z(j):
        def copy(up, z, src):
            return chain(src, wave(j, z), wzs.at[0 if up else 1, j, z], wzr.at[j, z], up)

        return copy

    def wave_y(j, z, e, src):
        return remote(src, wave(j, z), wys.at[j, e, z], wyr.at[j, e, z], me.device(y=e))

    def a_z(j):
        def copy(up, z, src):
            return chain(src, base(j, z), azs.at[0 if up else 1, j, z], azr.at[j, z], up)

        return copy

    def a_y(j, z, e, src):
        return remote(src, base(j, z), ays.at[j, e, z], ayr.at[j, e, z], me.device(y=e))

    def a_x(j, z, e, f, src):
        return remote(src, base(j, z, e), axs.at[j, f, e, z], axr.at[j, f, e, z], me.device(x=f))

    def b_y(j, e, src):
        return remote(src, base(j, me.z), bys.at[j, e], byr.at[j, e], me.device(y=e))

    def b_x(j, e, f, src):
        return remote(src, base(j, me.z, e), bxs.at[j, e, f], bxr.at[j, e, f], me.device(x=f))

    def b_z(j, f):
        def copy(up, z, src):
            return chain(
                src, base_strip(j, z, f), bzs.at[0 if up else 1, j, f, z], bzr.at[j, f, z], up
            )

        return copy

    def core(j, f, z):
        block = base_strip(j, z, f)
        return remote(block, block, kcs.at[j, f, z], kcr.at[j, f, z], me.device(c=1))

    def give_core(j, f, z):
        if nc > 1:
            core(j, f, z).start()

    def far_z(d, visit):
        @pl.when(me.z >= d)
        def _():
            visit(me.z - d, True)

        @pl.when(me.z + d < nz)
        def _():
            visit(me.z + d, False)

    def both_ways(start, src):
        @pl.when(me.z < nz - 1)
        def _():
            start(True, me.z, src).start()

        @pl.when(me.z > 0)
        def _():
            start(False, me.z, src).start()

    def relay(copy, block, z, up):
        copy(up, z, block).wait_recv()

        @pl.when(me.z < nz - 1 if up else me.z > 0)
        def _():
            copy(up, z, block).start()

    def sent_z(start, block):
        @pl.when(me.z < nz - 1)
        def _():
            @pl.loop(0, me.z + 1)
            def _(z):
                start(True, z, block(z)).wait_send()

        @pl.when(me.z > 0)
        def _():
            @pl.loop(me.z, nz)
            def _(z):
                start(False, z, block(z)).wait_send()

    def on_wave(z, up):
        for j in range(per_owner):
            block = wave(j, z)
            relay(wave_z(j), block, z, up)
            for e in range(1, ny):
                wave_y(j, z, e, block).start()

    def on_b_y():
        keep_base.wait()
        for j in odd:
            for e in range(1, ny):
                b_y(j, e, base(j, me.z, e)).wait_recv()
                for f in range(1, nx):
                    b_x(j, e, f, base(j, me.z, e)).start()

    me.greet()
    for j in odd:
        for e in range(1, ny):
            b_y(j, e, base_ref.at[j]).start()
    for j in range(per_owner):
        both_ways(wave_z(j), wave_ref.at[j])
        for e in range(1, ny):
            wave_y(j, me.z, e, wave_ref.at[j]).start()
    for f in range(1, nx):
        for j in odd:
            b_x(j, 0, f, base_ref.at[j]).start()
        for j in even:
            a_x(j, me.z, 0, f, base_ref.at[j]).start()
    keep_wave.start()
    keep_base.start()
    for copy in take_indices:
        copy.start()
    take_left.start()
    take_right.start()
    def a_start_z():
        for j in even:
            both_ways(a_z(j), base_ref.at[j])

    def a_start_y():
        for j in even:
            for e in range(1, ny):
                a_y(j, me.z, e, base_ref.at[j]).start()

    def on_a(z, up):
        for j in even:
            block = base(j, z)
            relay(a_z(j), block, z, up)
            for e in range(1, ny):
                a_y(j, z, e, block).start()
            for f in range(1, nx):
                a_x(j, z, 0, f, block).start()

    def on_b_x(f):
        for j in odd:
            if f:
                for e in range(ny):
                    b_x(j, e, f, base(j, me.z, e, f)).wait_recv()
            block = base_strip(j, me.z, f)
            both_ways(b_z(j, f), block)
            give_core(j, f, me.z)

    def on_b(f, z, up):
        for j in odd:
            block = base_strip(j, z, f)
            relay(b_z(j, f), block, z, up)
            give_core(j, f, z)

    def on_a_y(z, up=True):
        for j in even:
            for e in range(1, ny):
                block = base(j, z, e)
                a_y(j, z, e, block).wait_recv()
                for f in range(1, nx):
                    a_x(j, z, e, f, block).start()
            give_core(j, 0, z)

    def on_a_x(z, up=True):
        for j in even:
            for f in range(1, nx):
                for e in range(ny):
                    a_x(j, z, e, f, base(j, z, e, f)).wait_recv()
                give_core(j, f, z)

    def take_wave():
        keep_wave.wait()
        for copy in take_indices:
            copy.wait()
        take_left.wait()
        take_right.wait()
        for e in range(1, ny):

            @pl.loop(0, nz)
            def _(z):
                for j in range(per_owner):
                    wave_y(j, z, e, wave(j, z, e)).wait_recv()

        row = lax.broadcasted_iota(jnp.int32, (width, width), 0)
        column = lax.broadcasted_iota(jnp.int32, (width, width), 1)
        for j in range(per_owner):
            order = order_of(first + j, sector_slot, orders, sectors)
            inside = jnp.maximum(row, column) < order
            masked[j] = jnp.where(inside, wave_all[j], jnp.zeros((), bf16))

    def multiply(p, part):
        a = lax.rem(sector_slot[source[p]], per_owner)
        block = pl.ds(pl.multiple_of(part_of(part) * (deep * strip), strip), deep * strip)
        projected = jnp.dot(left[p, block, :], masked[a], preferred_element_type=f32)
        product[p, block, :] = lax.dot_general(
            projected.astype(bf16), right[p], (((1,), (1,)), ((), ())),
            preferred_element_type=f32,
        )

    def partial_sum(slot, start, size):
        landed = [sector_slot[target[p]] for p in range(count)]
        total = None
        for p in range(count):
            weight = jnp.where(landed[p] == slot, 1.0, 0.0).astype(f32)
            term = product[p, pl.ds(start, size), :] * weight
            total = term if total is None else total + term
        return total

    def axes(j):
        return ("x", "y") if j % 2 == 0 else ("y", "x")

    def core_copy(x, j, d):
        return remote(
            send_c.at[d, j, x], got_c.at[d, j, x], cs.at[d, j, x], cr.at[d, j, x], me.device(c=1)
        )

    def copy_1(j, d, k):
        return remote(
            send_1.at[d, j, k], got_1.at[d, j, k], s1.at[d, j, k], r1.at[d, j, k],
            me.device(**{axes(j)[0]: k}),
        )

    def copy_2(j, d, k):
        return remote(
            send_2.at[d, j, k], got_2.at[d, j, k], s2.at[d, j, k], r2.at[d, j, k],
            me.device(**{axes(j)[1]: k}),
        )

    def copy_3(j, d):
        return remote(
            send_3.at[d, j], got_3.at[d, j], s3.at[d, j], r3.at[d, j],
            me.device(z=lax.rem(z_of(d) - me.z + nz, nz)),
        )

    def stage_0(d):
        @pl.loop(0, per_owner * nx)
        def _(i):
            j, x = i // nx, lax.rem(i, nx)
            slot = (x * nc + lax.rem(me.c + 1, nc)) * per_owner + j
            for m in range(ny):
                value = partial_sum(slot, pl.multiple_of(z_of(d) * strip + m * slab, slab), slab)
                send_c[d, j, x, pl.ds(m * slab, slab), :] = value.astype(bf16)
            core_copy(x, j, d).start()

    def stage_1(d):
        for j in range(per_owner):
            n1 = size[axes(j)[0]]
            n2 = size[axes(j)[1]]
            if nc > 1:
                for x in range(nx):
                    core_copy(x, j, d).wait_recv()
            for k in list(range(1, n1)) + [0]:

                @pl.loop(0, n2)
                def _(m):
                    if axes(j)[0] == "x":
                        x, y = lax.rem(me.x + k, nx), m
                    else:
                        x, y = m, lax.rem(me.y + k, ny)
                    offset = pl.multiple_of(y * slab, slab)
                    slot = (x * nc + me.c) * per_owner + j
                    value = partial_sum(slot, pl.multiple_of(z_of(d) * strip + offset, slab), slab)
                    if nc > 1:
                        value = value + got_c[d, j, x, pl.ds(offset, slab), :].astype(f32)
                    if k:
                        send_1[d, j, k, m] = value.astype(bf16)
                    else:
                        mid[d, j, m] = value
                if k:
                    copy_1(j, d, k).start()

    def stage_2(d):
        for j in range(per_owner):
            axis_1, axis_2 = axes(j)
            n1, n2 = size[axis_1], size[axis_2]
            for k in range(1, n1):
                copy_1(j, d, k).wait_recv()
            for h in list(range(1, n2)) + [0]:
                m = lax.rem(getattr(me, axis_2) + h, n2)
                value = mid[d, j, m]
                for k in range(1, n1):
                    value = value + got_1[d, j, k, m].astype(f32)
                if h:
                    send_2[d, j, h] = value.astype(bf16)
                    copy_2(j, d, h).start()
                else:
                    held[d, j] = value

    def stage_3(d, j):
        for h in range(1, size[axes(j)[1]]):
            copy_2(j, d, h).wait_recv()
        value = held[d, j]
        for h in range(1, size[axes(j)[1]]):
            value = value + got_2[d, j, h].astype(f32)
        return value

    def stage_3_send(d):
        for j in range(per_owner):
            send_3[d, j] = stage_3(d, j).astype(bf16)
            copy_3(j, d).start()

    take_bases = pltpu.make_async_copy(
        base_all.at[pl.ds(first, per_owner)], own_bases, local.at[4]
    )

    def rotate_half():
        take_bases.start()
        take_bases.wait()
        for p in range(count):
            a = lax.rem(sector_slot[source[p]], per_owner)
            half[p] = jnp.dot(left[p], own_bases[a], preferred_element_type=f32).astype(bf16)

    def give_rotated(p):
        return pltpu.make_async_copy(right.at[p], rotated_hbm.at[p], give.at[p])

    def rotate():
        if nc > 1:
            for j in range(per_owner):
                for f in range(nx):

                    @pl.loop(0, nz)
                    def _(z):
                        core(j, f, z).wait_recv()

        for p in range(count):
            right[p] = lax.dot_general(
                base_all[sector_slot[target[p]]], half[p], (((0,), (0,)), ((), ())),
                preferred_element_type=f32,
            ).astype(bf16)
            give_rotated(p).start()

    def sent_bases():
        for j in range(per_owner):
            sent_z(wave_z(j), functools.partial(wave, j))

        @pl.loop(0, nz)
        def _(z):
            for j in range(per_owner):
                for e in range(1, ny):
                    wave_y(j, z, e, wave(j, z)).wait_send()
            for j in even:
                for e in range(1, ny):
                    a_y(j, z, e, base(j, z)).wait_send()
                for f in range(1, nx):
                    for e in range(ny):
                        a_x(j, z, e, f, base(j, z, e)).wait_send()

        for j in even:
            sent_z(a_z(j), functools.partial(base, j))
        for j in odd:
            for e in range(1, ny):
                b_y(j, e, base(j, me.z)).wait_send()
            for f in range(1, nx):
                for e in range(ny):
                    b_x(j, e, f, base(j, me.z, e)).wait_send()

    tasks = []

    def plan(key, visit, *args):
        tasks.append((key, len(tasks), visit, args))

    def after(key, *names):
        return max([key] + [done[name] for name in names])

    def step(name, d, f, needs, visit, *args):
        done[name, d, f] = after(timed(name, d, f), *needs)
        plan(done[name, d, f], visit, *args)

    done = {}
    for d in range(1, nz):
        plan(min(timed("wave", d), 0.0), far_z, d, on_wave)
    step("start_b_x", 0, 0, [], on_b_y)
    step("start_a_z", 0, 0, [], a_start_z)
    step("start_a_y", 0, 0, [("start_b_x", 0, 0)], a_start_y)
    for f in range(nx):
        step("start_b_z", 0, f, [("start_b_x", 0, 0)], on_b_x, f)
    for d in range(nz):
        before = ("a", d - 1, 0) if d > 1 else ("start_a_z", 0, 0)
        if d:
            step("a", d, 0, [before], far_z, d, on_a)
        for name, needs, visit in (
            ("a_y", ("a", d, 0) if d else ("start_a_y", 0, 0), on_a_y),
            ("a_x", ("a_y", d, 0), on_a_x),
        ):
            if d:
                step(name, d, 0, [needs], far_z, d, visit)
            else:
                step(name, d, 0, [needs], visit, me.z)
    for d in range(1, nz):
        for f in range(nx):
            before = ("b", d - 1, f) if d > 1 else ("start_b_z", 0, f)
            step("b", d, f, [before], far_z, d, functools.partial(on_b, f))
    bases = [name for name in done]
    plan(0.0, take_wave)
    for part in range(parts):
        for p in range(count):
            step("pair", p, part, [], multiply, p, part)
    for u in range(nz):
        needs = [("pair", count - 1, u // deep)]
        for name, visit in (
            ("stage_0", stage_0 if nc > 1 else None), ("stage_1", stage_1),
            ("stage_2", stage_2), ("stage_3", stage_3_send if u < nz - 1 else None),
        ):
            if visit:
                step(name, u, 0, needs + ([(name, u - 1, 0)] if u else []), visit, u)
                needs = [(name, u, 0)]
    own = [key for key in bases if key[0] in ("a_y", "b", "start_b_z") and key[2] == 0]
    step("half", 0, 0, own, rotate_half)
    step("rotate", 0, 0, bases + [("half", 0, 0)], rotate)
    for _, _, visit, args in sorted(tasks, key=lambda task: task[:2]):
        visit(*args)
    sent_bases()
    for j in odd:
        for f in range(nx):
            sent_z(b_z(j, f), lambda z: base_strip(j, z, f))
    if nc > 1:
        for j in range(per_owner):
            for f in range(nx):

                @pl.loop(0, nz)
                def _(z):
                    core(j, f, z).wait_send()

    @pl.loop(0, nz)
    def _(d):
        for j in range(per_owner):
            if nc > 1:
                for x in range(nx):
                    core_copy(x, j, d).wait_send()
            for k in range(1, size[axes(j)[0]]):
                copy_1(j, d, k).wait_send()
            for h in range(1, size[axes(j)[1]]):
                copy_2(j, d, h).wait_send()

    row = lax.broadcasted_iota(jnp.int32, (slab, width), 0) + (me.z * ny + me.y) * slab
    column = lax.broadcasted_iota(jnp.int32, (slab, width), 1)
    for j in range(per_owner):
        value = stage_3(nz - 1, j)
        for d in range(nz - 1):
            copy_3(j, d).wait_recv()
            value = value + got_3[d, j].astype(f32)
        order = order_of(first + j, sector_slot, orders, sectors)
        inside = jnp.maximum(row, column) < order
        out[j] = jnp.where(inside, value, 0.0).astype(out.dtype)

    for p in range(count):
        give_rotated(p).wait()
    @pl.loop(0, nz - 1)
    def _(d):
        for j in range(per_owner):
            copy_3(j, d).wait_send()


def sigma_and_rotation(
    dims, wavefunction, sector_bases, left, right, source, target, sector_slot, orders
):
    nx, nc, nz, ny = dims
    per_owner, slab, width = wavefunction.shape
    sectors = sector_slot.shape[0]
    most = max(nx, ny)
    dma = pltpu.SemaphoreType.DMA
    bf16, f32 = jnp.bfloat16, jnp.float32
    full = (per_owner, nz * ny * slab, width)
    return pl.pallas_call(
        functools.partial(sigma_kernel, dims, sectors),
        out_shape=(
            jax.ShapeDtypeStruct((per_owner, slab, width), bf16),
            jax.ShapeDtypeStruct(left.shape, bf16),
        ),
        in_specs=[ANY] * 8,
        out_specs=(VMEM, ANY),
        scratch_shapes=[
            pltpu.VMEM(full, bf16),
            pltpu.VMEM((sectors, nz * ny * slab, width), bf16),
            pltpu.VMEM(full, bf16),
            pltpu.VMEM(full, bf16),
            pltpu.VMEM(left.shape, bf16),
            pltpu.VMEM(left.shape, bf16),
            pltpu.VMEM(right.shape, bf16),
            pltpu.VMEM(left.shape, f32),
            pltpu.VMEM((nz, per_owner, nx, ny * slab, width), bf16),
            pltpu.VMEM((nz, per_owner, nx, ny * slab, width), bf16),
            pltpu.VMEM((nz, per_owner, most, most, slab, width), bf16),
            pltpu.VMEM((nz, per_owner, most, most, slab, width), bf16),
            pltpu.VMEM((nz, per_owner, most, slab, width), f32),
            pltpu.VMEM((nz, per_owner, most, slab, width), bf16),
            pltpu.VMEM((nz, per_owner, most, slab, width), bf16),
            pltpu.VMEM((nz, per_owner, slab, width), f32),
            pltpu.VMEM((nz, per_owner, slab, width), bf16),
            pltpu.VMEM((nz, per_owner, slab, width), bf16),
        ]
        + [dma((5,)), dma((left.shape[0],))]
        + [dma((2, per_owner, nz)), dma((per_owner, nz))]
        + [dma((per_owner, ny, nz))] * 2
        + [dma((2, per_owner, nz)), dma((per_owner, nz))]
        + [dma((per_owner, ny, nz))] * 2
        + [dma((per_owner, nx, ny, nz))] * 2
        + [dma((per_owner, ny))] * 2
        + [dma((per_owner, ny, nx))] * 2
        + [dma((2, per_owner, nx, nz)), dma((per_owner, nx, nz))]
        + [dma((per_owner, nx, nz))] * 2
        + [dma((nz, per_owner, nx))] * 2
        + [dma((nz, per_owner, most))] * 4
        + [dma((nz, per_owner))] * 2
        + [pltpu.SMEM(x.shape, x.dtype) for x in (source, target, sector_slot, orders)]
        + [dma((4,))],
        compiler_params=pltpu.CompilerParams(
            collective_id=0, has_side_effects=True, vmem_limit_bytes=60 * 1024 * 1024
        ),
        name="sigma",
    )(wavefunction, sector_bases, left, right, source, target, sector_slot, orders)


def hand_over_kernel(sigma, rotated, sigma_out, rotated_out, sigma_held, held, into, back):
    count = rotated.shape[0]

    def take(p):
        return pltpu.make_async_copy(rotated.at[p], held.at[p], into.at[p])

    def give(p):
        return pltpu.make_async_copy(held.at[p], rotated_out.at[p], back.at[p])

    take_sigma = pltpu.make_async_copy(sigma, sigma_held, into.at[count])
    give_sigma = pltpu.make_async_copy(sigma_held, sigma_out, back.at[count])
    for p in range(count):
        take(p).start()
    take_sigma.start()
    for p in range(count):
        take(p).wait()
        give(p).start()
    take_sigma.wait()
    give_sigma.start()
    for p in range(count):
        give(p).wait()
    give_sigma.wait()


def hand_over(sigma, rotated):
    count = rotated.shape[0]
    dma = pltpu.SemaphoreType.DMA
    return pl.pallas_call(
        hand_over_kernel,
        out_shape=(
            jax.ShapeDtypeStruct(sigma.shape, sigma.dtype),
            jax.ShapeDtypeStruct(rotated.shape, rotated.dtype),
        ),
        in_specs=[ANY, ANY],
        out_specs=(ANY, ANY),
        scratch_shapes=[
            pltpu.VMEM(sigma.shape, sigma.dtype),
            pltpu.VMEM(rotated.shape, rotated.dtype),
            dma((count + 1,)),
            dma((count + 1,)),
        ],
        compiler_params=pltpu.CompilerParams(vmem_limit_bytes=60 * 1024 * 1024),
        name="hand_over",
    )(sigma, rotated)


def solution(mesh):
    dims = grid_of(mesh.shape["sector"], mesh.shape["op"])

    def per_device(
        wavefunction, sector_bases, left_env, right_env, pair_source, pair_target, sector_slot, orders
    ):
        return hand_over(
            *sigma_and_rotation(
                dims, wavefunction, sector_bases, left_env, right_env,
                pair_source, pair_target, sector_slot, orders,
            )
        )

    placed = (
        P("sector", "op", None),
        P("sector", "op", None),
        P(("sector", "op"), None, None),
        P(("sector", "op"), None, None),
        P(("sector", "op")),
        P(("sector", "op")),
        P(),
        P(),
    )
    return jax.shard_map(
        per_device,
        mesh=mesh,
        in_specs=placed,
        out_specs=(P("sector", "op", None), P(("sector", "op"), None, None)),
        check_vma=False,
    )
```

```python
import functools

import jax
import jax.numpy as jnp
from jax import lax
from jax.experimental import pallas as pl
from jax.experimental.pallas import tpu as pltpu
from jax.sharding import PartitionSpec as P

MESH = pl.DeviceIdType.MESH
ANY = pl.BlockSpec(memory_space=pl.ANY)
VMEM = pl.BlockSpec(memory_space=pltpu.VMEM)
SMEM = pl.BlockSpec(memory_space=pltpu.SMEM)


def grid_of(n_sector, n_op):
    cores = 2 if n_sector % 2 == 0 else 1
    ny = 1
    while ny * ny * 4 <= n_op and n_op % (ny * 2) == 0:
        ny *= 2
    return n_sector // cores, cores, n_op // ny, ny


class Place:
    def __init__(self, dims):
        self.dims = dims
        nx, nc, nz, ny = dims
        sector, op = lax.axis_index("sector"), lax.axis_index("op")
        self.x, self.c = sector // nc, sector % nc
        self.z, self.y = op // ny, op % ny

    def at(self, x=0, c=0, z=0, y=0):
        nx, nc, nz, ny = self.dims
        return (
            lax.rem(self.x + x, nx),
            lax.rem(self.c + c, nc),
            lax.rem(self.z + z, nz),
            lax.rem(self.y + y, ny),
        )

    def device(self, **shift):
        nx, nc, nz, ny = self.dims
        x, c, z, y = self.at(**shift)
        return (x * nc + c, z * ny + y)

    def greet(self):
        barrier = pltpu.get_barrier_semaphore()
        nx, nc, nz, ny = self.dims
        count = 0
        for name, n in (("x", nx), ("c", nc), ("y", ny)):
            for shift in range(1, n):
                pl.semaphore_signal(
                    barrier, inc=1, device_id=self.device(**{name: shift}), device_id_type=MESH
                )
                count += 1
        for there, shift in ((self.z < nz - 1, 1), (self.z > 0, nz - 1)):

            @pl.when(there)
            def _():
                pl.semaphore_signal(
                    barrier, inc=1, device_id=self.device(z=shift), device_id_type=MESH
                )

        count = count + (self.z < nz - 1).astype(jnp.int32) + (self.z > 0).astype(jnp.int32)
        pl.semaphore_wait(barrier, count)


def remote(src, dst, send, recv, device):
    return pltpu.make_async_remote_copy(
        src_ref=src, dst_ref=dst, send_sem=send, recv_sem=recv, device_id=device, device_id_type=MESH
    )


def order_of(slot, sector_slot, orders, sectors):
    total = jnp.int32(0)
    for i in range(sectors):
        total = total + jnp.where(sector_slot[i] == slot, orders[i], 0)
    return total


PLAN = {
    "wave": ((-8, -8, -7, -6),),
    "a": ((-4, -4, -3, -1),),
    "a_y": ((31, 5, 10, 13),),
    "a_x": ((35, 38, 39, 36),),
    "b": ((12, 12, 26, 32), (20, 20, 29, 41)),
    "start_b_x": ((-5,),),
    "start_b_z": ((-2,), (8,)),
    "start_a_z": ((-9,),),
    "start_a_y": ((11,),),
    "pair": ((1, 2, 3, 4, 6, 7), (15, 17, 19, 21, 22, 23)),
    "stage_0": ((9, 14, 24, 27),),
    "stage_1": ((16, 18, 28, 37),),
    "stage_2": ((25, 33, 34, 44),),
    "stage_3": ((30, 40, 42, 46),),
    "half": ((43,),),
    "rotate": ((45,),),
}


def timed(name, d=0, f=0):
    row = PLAN[name][min(f, len(PLAN[name]) - 1)]
    beyond = max(d - len(row) + 1, 0)
    return float(row[min(d, len(row) - 1)] + beyond * (row[-1] - row[max(len(row) - 2, 0)]))


def sigma_kernel(
    dims, sectors, wave_ref, base_ref, left_hbm, right_hbm,
    source_hbm, target_hbm, sector_slot_hbm, orders_hbm,
    out, rotated_hbm,
    wave_all, base_all, masked, own_bases, half, left, right, product,
    send_c, got_c, send_1, got_1, mid, send_2, got_2, held, send_3, got_3,
    local, give, wzs, wzr, wys, wyr, azs, azr, ays, ayr, axs, axr,
    bys, byr, bxs, bxr, bzs, bzr, kcs, kcr,
    cs, cr, s1, r1, s2, r2, s3, r3,
    source, target, sector_slot, orders, indices,
):
    nx, nc, nz, ny = dims
    me = Place(dims)
    per_owner, slab, width = out.shape
    count = left.shape[0]
    strip = ny * slab
    f32, bf16 = jnp.float32, jnp.bfloat16
    size = {"x": nx, "y": ny}
    first = (me.x * nc + me.c) * per_owner
    parts = 2 if nz % 2 == 0 else 1
    deep = nz // parts
    even = list(range(0, per_owner, 2))
    odd = list(range(1, per_owner, 2))

    def rows(z, y):
        return pl.ds((z * ny + y) * slab, slab)

    def wave(j, z, e=0):
        return wave_all.at[j, rows(z, lax.rem(me.y + ny - e, ny)), :]

    def part_of(part):
        return lax.rem(me.z // deep + 1 + part, parts)

    def z_of(u):
        part, step = u // deep, u % deep
        step = step + part + 2 - parts
        return part_of(part) * deep + lax.rem(me.z + step, deep)

    def slot_of(j, f, g=0):
        x, c, _, _ = me.at(x=nx - f, c=nc - g)
        return (x * nc + c) * per_owner + j

    def base(j, z, e=0, f=0):
        return base_all.at[slot_of(j, f), rows(z, lax.rem(me.y + ny - e, ny)), :]

    def base_strip(j, z, f, g=0):
        return base_all.at[slot_of(j, f, g), pl.ds(z * strip, strip), :]

    keep_wave = pltpu.make_async_copy(
        wave_ref, wave_all.at[:, rows(me.z, me.y), :], local.at[0]
    )
    keep_base = pltpu.make_async_copy(
        base_ref, base_all.at[pl.ds(first, per_owner), rows(me.z, me.y), :], local.at[1]
    )
    take_left = pltpu.make_async_copy(left_hbm, left, local.at[2])
    take_indices = [
        pltpu.make_async_copy(there, here, indices.at[i])
        for i, (there, here) in enumerate(
            (
                (source_hbm, source), (target_hbm, target),
                (sector_slot_hbm, sector_slot), (orders_hbm, orders),
            )
        )
    ]
    take_right = pltpu.make_async_copy(right_hbm, right, local.at[3])

    def chain(src, dst, send, recv, up):
        return remote(src, dst, send, recv, me.device(z=1 if up else nz - 1))

    def wave_z(j):
        def copy(up, z, src):
            return chain(src, wave(j, z), wzs.at[0 if up else 1, j, z], wzr.at[j, z], up)

        return copy

    def wave_y(j, z, e, src):
        return remote(src, wave(j, z), wys.at[j, e, z], wyr.at[j, e, z], me.device(y=e))

    def a_z(j):
        def copy(up, z, src):
            return chain(src, base(j, z), azs.at[0 if up else 1, j, z], azr.at[j, z], up)

        return copy

    def a_y(j, z, e, src):
        return remote(src, base(j, z), ays.at[j, e, z], ayr.at[j, e, z], me.device(y=e))

    def a_x(j, z, e, f, src):
        return remote(src, base(j, z, e), axs.at[j, f, e, z], axr.at[j, f, e, z], me.device(x=f))

    def b_y(j, e, src):
        return remote(src, base(j, me.z), bys.at[j, e], byr.at[j, e], me.device(y=e))

    def b_x(j, e, f, src):
        return remote(src, base(j, me.z, e), bxs.at[j, e, f], bxr.at[j, e, f], me.device(x=f))

    def b_z(j, f):
        def copy(up, z, src):
            return chain(
                src, base_strip(j, z, f), bzs.at[0 if up else 1, j, f, z], bzr.at[j, f, z], up
            )

        return copy

    def core(j, f, z):
        block = base_strip(j, z, f)
        return remote(block, block, kcs.at[j, f, z], kcr.at[j, f, z], me.device(c=1))

    def give_core(j, f, z):
        if nc > 1:
            core(j, f, z).start()

    def far_z(d, visit):
        @pl.when(me.z >= d)
        def _():
            visit(me.z - d, True)

        @pl.when(me.z + d < nz)
        def _():
            visit(me.z + d, False)

    def both_ways(start, src):
        @pl.when(me.z < nz - 1)
        def _():
            start(True, me.z, src).start()

        @pl.when(me.z > 0)
        def _():
            start(False, me.z, src).start()

    def relay(copy, block, z, up):
        copy(up, z, block).wait_recv()

        @pl.when(me.z < nz - 1 if up else me.z > 0)
        def _():
            copy(up, z, block).start()

    def sent_z(start, block):
        @pl.when(me.z < nz - 1)
        def _():
            @pl.loop(0, me.z + 1)
            def _(z):
                start(True, z, block(z)).wait_send()

        @pl.when(me.z > 0)
        def _():
            @pl.loop(me.z, nz)
            def _(z):
                start(False, z, block(z)).wait_send()

    def on_wave(z, up):
        for j in range(per_owner):
            block = wave(j, z)
            relay(wave_z(j), block, z, up)
            for e in range(1, ny):
                wave_y(j, z, e, block).start()

    def on_b_y():
        keep_base.wait()
        for j in odd:
            for e in range(1, ny):
                b_y(j, e, base(j, me.z, e)).wait_recv()
                for f in range(1, nx):
                    b_x(j, e, f, base(j, me.z, e)).start()

    me.greet()
    for j in odd:
        for e in range(1, ny):
            b_y(j, e, base_ref.at[j]).start()
    for j in range(per_owner):
        both_ways(wave_z(j), wave_ref.at[j])
        for e in range(1, ny):
            wave_y(j, me.z, e, wave_ref.at[j]).start()
    for f in range(1, nx):
        for j in odd:
            b_x(j, 0, f, base_ref.at[j]).start()
        for j in even:
            a_x(j, me.z, 0, f, base_ref.at[j]).start()
    keep_wave.start()
    keep_base.start()
    for copy in take_indices:
        copy.start()
    take_left.start()
    take_right.start()
    def a_start_z():
        for j in even:
            both_ways(a_z(j), base_ref.at[j])

    def a_start_y():
        for j in even:
            for e in range(1, ny):
                a_y(j, me.z, e, base_ref.at[j]).start()

    def on_a(z, up):
        for j in even:
            block = base(j, z)
            relay(a_z(j), block, z, up)
            for e in range(1, ny):
                a_y(j, z, e, block).start()
            for f in range(1, nx):
                a_x(j, z, 0, f, block).start()

    def on_b_x(f):
        for j in odd:
            if f:
                for e in range(ny):
                    b_x(j, e, f, base(j, me.z, e, f)).wait_recv()
            block = base_strip(j, me.z, f)
            both_ways(b_z(j, f), block)
            give_core(j, f, me.z)

    def on_b(f, z, up):
        for j in odd:
            block = base_strip(j, z, f)
            relay(b_z(j, f), block, z, up)
            give_core(j, f, z)

    def on_a_y(z, up=True):
        for j in even:
            for e in range(1, ny):
                block = base(j, z, e)
                a_y(j, z, e, block).wait_recv()
                for f in range(1, nx):
                    a_x(j, z, e, f, block).start()
            give_core(j, 0, z)

    def on_a_x(z, up=True):
        for j in even:
            for f in range(1, nx):
                for e in range(ny):
                    a_x(j, z, e, f, base(j, z, e, f)).wait_recv()
                give_core(j, f, z)

    def take_wave():
        keep_wave.wait()
        for copy in take_indices:
            copy.wait()
        take_left.wait()
        take_right.wait()
        for e in range(1, ny):

            @pl.loop(0, nz)
            def _(z):
                for j in range(per_owner):
                    wave_y(j, z, e, wave(j, z, e)).wait_recv()

        row = lax.broadcasted_iota(jnp.int32, (width, width), 0)
        column = lax.broadcasted_iota(jnp.int32, (width, width), 1)
        for j in range(per_owner):
            order = order_of(first + j, sector_slot, orders, sectors)
            inside = jnp.maximum(row, column) < order
            masked[j] = jnp.where(inside, wave_all[j], jnp.zeros((), bf16))

    def multiply(p, part):
        a = lax.rem(sector_slot[source[p]], per_owner)
        block = pl.ds(pl.multiple_of(part_of(part) * (deep * strip), strip), deep * strip)
        projected = jnp.dot(left[p, block, :], masked[a], preferred_element_type=f32)
        product[p, block, :] = lax.dot_general(
            projected.astype(bf16), right[p], (((1,), (1,)), ((), ())),
            preferred_element_type=f32,
        )

    def partial_sum(slot, start, size):
        landed = [sector_slot[target[p]] for p in range(count)]
        total = None
        for p in range(count):
            weight = jnp.where(landed[p] == slot, 1.0, 0.0).astype(f32)
            term = product[p, pl.ds(start, size), :] * weight
            total = term if total is None else total + term
        return total

    def axes(j):
        return ("x", "y") if j % 2 == 0 else ("y", "x")

    def core_copy(x, j, d):
        return remote(
            send_c.at[d, j, x], got_c.at[d, j, x], cs.at[d, j, x], cr.at[d, j, x], me.device(c=1)
        )

    def copy_1(j, d, k):
        return remote(
            send_1.at[d, j, k], got_1.at[d, j, k], s1.at[d, j, k], r1.at[d, j, k],
            me.device(**{axes(j)[0]: k}),
        )

    def copy_2(j, d, k):
        return remote(
            send_2.at[d, j, k], got_2.at[d, j, k], s2.at[d, j, k], r2.at[d, j, k],
            me.device(**{axes(j)[1]: k}),
        )

    def copy_3(j, d):
        return remote(
            send_3.at[d, j], got_3.at[d, j], s3.at[d, j], r3.at[d, j],
            me.device(z=lax.rem(z_of(d) - me.z + nz, nz)),
        )

    def stage_0(d):
        @pl.loop(0, per_owner * nx)
        def _(i):
            j, x = i // nx, lax.rem(i, nx)
            slot = (x * nc + lax.rem(me.c + 1, nc)) * per_owner + j
            for m in range(ny):
                value = partial_sum(slot, pl.multiple_of(z_of(d) * strip + m * slab, slab), slab)
                send_c[d, j, x, pl.ds(m * slab, slab), :] = value.astype(bf16)
            core_copy(x, j, d).start()

    def stage_1(d):
        for j in range(per_owner):
            n1 = size[axes(j)[0]]
            n2 = size[axes(j)[1]]
            if nc > 1:
                for x in range(nx):
                    core_copy(x, j, d).wait_recv()
            for k in list(range(1, n1)) + [0]:

                @pl.loop(0, n2)
                def _(m):
                    if axes(j)[0] == "x":
                        x, y = lax.rem(me.x + k, nx), m
                    else:
                        x, y = m, lax.rem(me.y + k, ny)
                    offset = pl.multiple_of(y * slab, slab)
                    slot = (x * nc + me.c) * per_owner + j
                    value = partial_sum(slot, pl.multiple_of(z_of(d) * strip + offset, slab), slab)
                    if nc > 1:
                        value = value + got_c[d, j, x, pl.ds(offset, slab), :].astype(f32)
                    if k:
                        send_1[d, j, k, m] = value.astype(bf16)
                    else:
                        mid[d, j, m] = value
                if k:
                    copy_1(j, d, k).start()

    def stage_2(d):
        for j in range(per_owner):
            axis_1, axis_2 = axes(j)
            n1, n2 = size[axis_1], size[axis_2]
            for k in range(1, n1):
                copy_1(j, d, k).wait_recv()
            for h in list(range(1, n2)) + [0]:
                m = lax.rem(getattr(me, axis_2) + h, n2)
                value = mid[d, j, m]
                for k in range(1, n1):
                    value = value + got_1[d, j, k, m].astype(f32)
                if h:
                    send_2[d, j, h] = value.astype(bf16)
                    copy_2(j, d, h).start()
                else:
                    held[d, j] = value

    def stage_3(d, j):
        for h in range(1, size[axes(j)[1]]):
            copy_2(j, d, h).wait_recv()
        value = held[d, j]
        for h in range(1, size[axes(j)[1]]):
            value = value + got_2[d, j, h].astype(f32)
        return value

    def stage_3_send(d):
        for j in range(per_owner):
            send_3[d, j] = stage_3(d, j).astype(bf16)
            copy_3(j, d).start()

    take_bases = pltpu.make_async_copy(
        base_all.at[pl.ds(first, per_owner)], own_bases, local.at[4]
    )

    def rotate_half():
        take_bases.start()
        take_bases.wait()
        for p in range(count):
            a = lax.rem(sector_slot[source[p]], per_owner)
            half[p] = jnp.dot(left[p], own_bases[a], preferred_element_type=f32).astype(bf16)

    def give_rotated(p):
        return pltpu.make_async_copy(right.at[p], rotated_hbm.at[p], give.at[p])

    def rotate():
        if nc > 1:
            for j in range(per_owner):
                for f in range(nx):

                    @pl.loop(0, nz)
                    def _(z):
                        core(j, f, z).wait_recv()

        for p in range(count):
            right[p] = lax.dot_general(
                base_all[sector_slot[target[p]]], half[p], (((0,), (0,)), ((), ())),
                preferred_element_type=f32,
            ).astype(bf16)
            give_rotated(p).start()

    def sent_bases():
        for j in range(per_owner):
            sent_z(wave_z(j), functools.partial(wave, j))

        @pl.loop(0, nz)
        def _(z):
            for j in range(per_owner):
                for e in range(1, ny):
                    wave_y(j, z, e, wave(j, z)).wait_send()
            for j in even:
                for e in range(1, ny):
                    a_y(j, z, e, base(j, z)).wait_send()
                for f in range(1, nx):
                    for e in range(ny):
                        a_x(j, z, e, f, base(j, z, e)).wait_send()

        for j in even:
            sent_z(a_z(j), functools.partial(base, j))
        for j in odd:
            for e in range(1, ny):
                b_y(j, e, base(j, me.z)).wait_send()
            for f in range(1, nx):
                for e in range(ny):
                    b_x(j, e, f, base(j, me.z, e)).wait_send()

    tasks = []

    def plan(key, visit, *args):
        tasks.append((key, len(tasks), visit, args))

    def after(key, *names):
        return max([key] + [done[name] for name in names])

    def step(name, d, f, needs, visit, *args):
        done[name, d, f] = after(timed(name, d, f), *needs)
        plan(done[name, d, f], visit, *args)

    done = {}
    for d in range(1, nz):
        plan(min(timed("wave", d), 0.0), far_z, d, on_wave)
    step("start_b_x", 0, 0, [], on_b_y)
    step("start_a_z", 0, 0, [], a_start_z)
    step("start_a_y", 0, 0, [("start_b_x", 0, 0)], a_start_y)
    for f in range(nx):
        step("start_b_z", 0, f, [("start_b_x", 0, 0)], on_b_x, f)
    for d in range(nz):
        before = ("a", d - 1, 0) if d > 1 else ("start_a_z", 0, 0)
        if d:
            step("a", d, 0, [before], far_z, d, on_a)
        for name, needs, visit in (
            ("a_y", ("a", d, 0) if d else ("start_a_y", 0, 0), on_a_y),
            ("a_x", ("a_y", d, 0), on_a_x),
        ):
            if d:
                step(name, d, 0, [needs], far_z, d, visit)
            else:
                step(name, d, 0, [needs], visit, me.z)
    for d in range(1, nz):
        for f in range(nx):
            before = ("b", d - 1, f) if d > 1 else ("start_b_z", 0, f)
            step("b", d, f, [before], far_z, d, functools.partial(on_b, f))
    bases = [name for name in done]
    plan(0.0, take_wave)
    for part in range(parts):
        for p in range(count):
            step("pair", p, part, [], multiply, p, part)
    for u in range(nz):
        needs = [("pair", count - 1, u // deep)]
        for name, visit in (
            ("stage_0", stage_0 if nc > 1 else None), ("stage_1", stage_1),
            ("stage_2", stage_2), ("stage_3", stage_3_send if u < nz - 1 else None),
        ):
            if visit:
                step(name, u, 0, needs + ([(name, u - 1, 0)] if u else []), visit, u)
                needs = [(name, u, 0)]
    own = [key for key in bases if key[0] in ("a_y", "b", "start_b_z") and key[2] == 0]
    step("half", 0, 0, own, rotate_half)
    step("rotate", 0, 0, bases + [("half", 0, 0)], rotate)
    for _, _, visit, args in sorted(tasks, key=lambda task: task[:2]):
        visit(*args)
    sent_bases()
    for j in odd:
        for f in range(nx):
            sent_z(b_z(j, f), lambda z: base_strip(j, z, f))
    if nc > 1:
        for j in range(per_owner):
            for f in range(nx):

                @pl.loop(0, nz)
                def _(z):
                    core(j, f, z).wait_send()

    @pl.loop(0, nz)
    def _(d):
        for j in range(per_owner):
            if nc > 1:
                for x in range(nx):
                    core_copy(x, j, d).wait_send()
            for k in range(1, size[axes(j)[0]]):
                copy_1(j, d, k).wait_send()
            for h in range(1, size[axes(j)[1]]):
                copy_2(j, d, h).wait_send()

    row = lax.broadcasted_iota(jnp.int32, (slab, width), 0) + (me.z * ny + me.y) * slab
    column = lax.broadcasted_iota(jnp.int32, (slab, width), 1)
    for j in range(per_owner):
        value = stage_3(nz - 1, j)
        for d in range(nz - 1):
            copy_3(j, d).wait_recv()
            value = value + got_3[d, j].astype(f32)
        order = order_of(first + j, sector_slot, orders, sectors)
        inside = jnp.maximum(row, column) < order
        out[j] = jnp.where(inside, value, 0.0).astype(out.dtype)

    for p in range(count):
        give_rotated(p).wait()
    @pl.loop(0, nz - 1)
    def _(d):
        for j in range(per_owner):
            copy_3(j, d).wait_send()


def sigma_and_rotation(
    dims, wavefunction, sector_bases, left, right, source, target, sector_slot, orders
):
    nx, nc, nz, ny = dims
    per_owner, slab, width = wavefunction.shape
    sectors = sector_slot.shape[0]
    most = max(nx, ny)
    dma = pltpu.SemaphoreType.DMA
    bf16, f32 = jnp.bfloat16, jnp.float32
    full = (per_owner, nz * ny * slab, width)
    return pl.pallas_call(
        functools.partial(sigma_kernel, dims, sectors),
        out_shape=(
            jax.ShapeDtypeStruct((per_owner, slab, width), bf16),
            jax.ShapeDtypeStruct(left.shape, bf16),
        ),
        in_specs=[ANY] * 8,
        out_specs=(VMEM, ANY),
        scratch_shapes=[
            pltpu.VMEM(full, bf16),
            pltpu.VMEM((sectors, nz * ny * slab, width), bf16),
            pltpu.VMEM(full, bf16),
            pltpu.VMEM(full, bf16),
            pltpu.VMEM(left.shape, bf16),
            pltpu.VMEM(left.shape, bf16),
            pltpu.VMEM(right.shape, bf16),
            pltpu.VMEM(left.shape, f32),
            pltpu.VMEM((nz, per_owner, nx, ny * slab, width), bf16),
            pltpu.VMEM((nz, per_owner, nx, ny * slab, width), bf16),
            pltpu.VMEM((nz, per_owner, most, most, slab, width), bf16),
            pltpu.VMEM((nz, per_owner, most, most, slab, width), bf16),
            pltpu.VMEM((nz, per_owner, most, slab, width), f32),
            pltpu.VMEM((nz, per_owner, most, slab, width), bf16),
            pltpu.VMEM((nz, per_owner, most, slab, width), bf16),
            pltpu.VMEM((nz, per_owner, slab, width), f32),
            pltpu.VMEM((nz, per_owner, slab, width), bf16),
            pltpu.VMEM((nz, per_owner, slab, width), bf16),
        ]
        + [dma((5,)), dma((left.shape[0],))]
        + [dma((2, per_owner, nz)), dma((per_owner, nz))]
        + [dma((per_owner, ny, nz))] * 2
        + [dma((2, per_owner, nz)), dma((per_owner, nz))]
        + [dma((per_owner, ny, nz))] * 2
        + [dma((per_owner, nx, ny, nz))] * 2
        + [dma((per_owner, ny))] * 2
        + [dma((per_owner, ny, nx))] * 2
        + [dma((2, per_owner, nx, nz)), dma((per_owner, nx, nz))]
        + [dma((per_owner, nx, nz))] * 2
        + [dma((nz, per_owner, nx))] * 2
        + [dma((nz, per_owner, most))] * 4
        + [dma((nz, per_owner))] * 2
        + [pltpu.SMEM(x.shape, x.dtype) for x in (source, target, sector_slot, orders)]
        + [dma((4,))],
        compiler_params=pltpu.CompilerParams(
            collective_id=0, has_side_effects=True, vmem_limit_bytes=60 * 1024 * 1024
        ),
        name="sigma",
    )(wavefunction, sector_bases, left, right, source, target, sector_slot, orders)


def hand_over_kernel(sigma, rotated, sigma_out, rotated_out, sigma_held, held, into, back):
    count = rotated.shape[0]

    def take(p):
        return pltpu.make_async_copy(rotated.at[p], held.at[p], into.at[p])

    def give(p):
        return pltpu.make_async_copy(held.at[p], rotated_out.at[p], back.at[p])

    take_sigma = pltpu.make_async_copy(sigma, sigma_held, into.at[count])
    give_sigma = pltpu.make_async_copy(sigma_held, sigma_out, back.at[count])
    for p in range(count):
        take(p).start()
    take_sigma.start()
    for p in range(count):
        take(p).wait()
        give(p).start()
    take_sigma.wait()
    give_sigma.start()
    for p in range(count):
        give(p).wait()
    give_sigma.wait()


def hand_over(sigma, rotated):
    count = rotated.shape[0]
    dma = pltpu.SemaphoreType.DMA
    return pl.pallas_call(
        hand_over_kernel,
        out_shape=(
            jax.ShapeDtypeStruct(sigma.shape, sigma.dtype),
            jax.ShapeDtypeStruct(rotated.shape, rotated.dtype),
        ),
        in_specs=[ANY, ANY],
        out_specs=(ANY, ANY),
        scratch_shapes=[
            pltpu.VMEM(sigma.shape, sigma.dtype),
            pltpu.VMEM(rotated.shape, rotated.dtype),
            dma((count + 1,)),
            dma((count + 1,)),
        ],
        compiler_params=pltpu.CompilerParams(vmem_limit_bytes=60 * 1024 * 1024),
        name="hand_over",
    )(sigma, rotated)


def solution(mesh):
    dims = grid_of(mesh.shape["sector"], mesh.shape["op"])

    def per_device(
        wavefunction, sector_bases, left_env, right_env, pair_source, pair_target, sector_slot, orders
    ):
        return hand_over(
            *sigma_and_rotation(
                dims, wavefunction, sector_bases, left_env, right_env,
                pair_source, pair_target, sector_slot, orders,
            )
        )

    placed = (
        P("sector", "op", None),
        P("sector", "op", None),
        P(("sector", "op"), None, None),
        P(("sector", "op"), None, None),
        P(("sector", "op")),
        P(("sector", "op")),
        P(),
        P(),
    )
    return jax.shard_map(
        per_device,
        mesh=mesh,
        in_specs=placed,
        out_specs=(P("sector", "op", None), P(("sector", "op"), None, None)),
        check_vma=False,
    )
```

```python
import functools

import jax
import jax.numpy as jnp
from jax import lax
from jax.experimental import pallas as pl
from jax.experimental.pallas import tpu as pltpu
from jax.sharding import PartitionSpec as P

MESH = pl.DeviceIdType.MESH
ANY = pl.BlockSpec(memory_space=pl.ANY)
VMEM = pl.BlockSpec(memory_space=pltpu.VMEM)
SMEM = pl.BlockSpec(memory_space=pltpu.SMEM)


def grid_of(n_sector, n_op):
    cores = 2 if n_sector % 2 == 0 else 1
    ny = 1
    while ny * ny * 4 <= n_op and n_op % (ny * 2) == 0:
        ny *= 2
    return n_sector // cores, cores, n_op // ny, ny


class Place:
    def __init__(self, dims):
        self.dims = dims
        nx, nc, nz, ny = dims
        sector, op = lax.axis_index("sector"), lax.axis_index("op")
        self.x, self.c = sector // nc, sector % nc
        self.z, self.y = op // ny, op % ny

    def at(self, x=0, c=0, z=0, y=0):
        nx, nc, nz, ny = self.dims
        return (
            lax.rem(self.x + x, nx),
            lax.rem(self.c + c, nc),
            lax.rem(self.z + z, nz),
            lax.rem(self.y + y, ny),
        )

    def device(self, **shift):
        nx, nc, nz, ny = self.dims
        x, c, z, y = self.at(**shift)
        return (x * nc + c, z * ny + y)

    def greet(self):
        barrier = pltpu.get_barrier_semaphore()
        nx, nc, nz, ny = self.dims
        count = 0
        for name, n in (("x", nx), ("c", nc), ("y", ny)):
            for shift in range(1, n):
                pl.semaphore_signal(
                    barrier, inc=1, device_id=self.device(**{name: shift}), device_id_type=MESH
                )
                count += 1
        for there, shift in ((self.z < nz - 1, 1), (self.z > 0, nz - 1)):

            @pl.when(there)
            def _():
                pl.semaphore_signal(
                    barrier, inc=1, device_id=self.device(z=shift), device_id_type=MESH
                )

        count = count + (self.z < nz - 1).astype(jnp.int32) + (self.z > 0).astype(jnp.int32)
        pl.semaphore_wait(barrier, count)


def remote(src, dst, send, recv, device):
    return pltpu.make_async_remote_copy(
        src_ref=src, dst_ref=dst, send_sem=send, recv_sem=recv, device_id=device, device_id_type=MESH
    )


def order_of(slot, sector_slot, orders, sectors):
    total = jnp.int32(0)
    for i in range(sectors):
        total = total + jnp.where(sector_slot[i] == slot, orders[i], 0)
    return total


PLAN = {
    "wave": ((-8, -8, -7, -6),),
    "a": ((-4, -4, -3, -1),),
    "a_y": ((31, 5, 10, 13),),
    "a_x": ((35, 38, 39, 36),),
    "b": ((12, 12, 26, 32), (20, 20, 29, 41)),
    "start_b_x": ((-5,),),
    "start_b_z": ((-2,), (8,)),
    "start_a_z": ((-9,),),
    "start_a_y": ((11,),),
    "pair": ((1, 2, 3, 4, 6, 7), (15, 17, 19, 21, 22, 23)),
    "stage_0": ((9, 14, 24, 27),),
    "stage_1": ((16, 18, 28, 37),),
    "stage_2": ((25, 33, 34, 44),),
    "stage_3": ((30, 40, 42, 46),),
    "half": ((43,),),
    "rotate": ((45,),),
}


def timed(name, d=0, f=0):
    row = PLAN[name][min(f, len(PLAN[name]) - 1)]
    beyond = max(d - len(row) + 1, 0)
    return float(row[min(d, len(row) - 1)] + beyond * (row[-1] - row[max(len(row) - 2, 0)]))


def sigma_kernel(
    dims, sectors, wave_ref, base_ref, left_hbm, right_hbm,
    source_hbm, target_hbm, sector_slot_hbm, orders_hbm,
    out, rotated_hbm,
    wave_all, base_all, masked, own_bases, half, left, right, product,
    send_c, got_c, send_1, got_1, mid, send_2, got_2, held, send_3, got_3,
    local, give, wzs, wzr, wys, wyr, azs, azr, ays, ayr, axs, axr,
    bys, byr, bxs, bxr, bzs, bzr, kcs, kcr,
    cs, cr, s1, r1, s2, r2, s3, r3,
    source, target, sector_slot, orders, indices,
):
    nx, nc, nz, ny = dims
    me = Place(dims)
    per_owner, slab, width = out.shape
    count = left.shape[0]
    strip = ny * slab
    f32, bf16 = jnp.float32, jnp.bfloat16
    size = {"x": nx, "y": ny}
    first = (me.x * nc + me.c) * per_owner
    parts = 2 if nz % 2 == 0 else 1
    deep = nz // parts
    even = list(range(0, per_owner, 2))
    odd = list(range(1, per_owner, 2))

    def rows(z, y):
        return pl.ds((z * ny + y) * slab, slab)

    def wave(j, z, e=0):
        return wave_all.at[j, rows(z, lax.rem(me.y + ny - e, ny)), :]

    def part_of(part):
        return lax.rem(me.z // deep + 1 + part, parts)

    def z_of(u):
        part, step = u // deep, u % deep
        step = step + part + 2 - parts
        return part_of(part) * deep + lax.rem(me.z + step, deep)

    def slot_of(j, f, g=0):
        x, c, _, _ = me.at(x=nx - f, c=nc - g)
        return (x * nc + c) * per_owner + j

    def base(j, z, e=0, f=0):
        return base_all.at[slot_of(j, f), rows(z, lax.rem(me.y + ny - e, ny)), :]

    def base_strip(j, z, f, g=0):
        return base_all.at[slot_of(j, f, g), pl.ds(z * strip, strip), :]

    keep_wave = pltpu.make_async_copy(
        wave_ref, wave_all.at[:, rows(me.z, me.y), :], local.at[0]
    )
    keep_base = pltpu.make_async_copy(
        base_ref, base_all.at[pl.ds(first, per_owner), rows(me.z, me.y), :], local.at[1]
    )
    take_left = pltpu.make_async_copy(left_hbm, left, local.at[2])
    take_indices = [
        pltpu.make_async_copy(there, here, indices.at[i])
        for i, (there, here) in enumerate(
            (
                (source_hbm, source), (target_hbm, target),
                (sector_slot_hbm, sector_slot), (orders_hbm, orders),
            )
        )
    ]
    take_right = pltpu.make_async_copy(right_hbm, right, local.at[3])

    def chain(src, dst, send, recv, up):
        return remote(src, dst, send, recv, me.device(z=1 if up else nz - 1))

    def wave_z(j):
        def copy(up, z, src):
            return chain(src, wave(j, z), wzs.at[0 if up else 1, j, z], wzr.at[j, z], up)

        return copy

    def wave_y(j, z, e, src):
        return remote(src, wave(j, z), wys.at[j, e, z], wyr.at[j, e, z], me.device(y=e))

    def a_z(j):
        def copy(up, z, src):
            return chain(src, base(j, z), azs.at[0 if up else 1, j, z], azr.at[j, z], up)

        return copy

    def a_y(j, z, e, src):
        return remote(src, base(j, z), ays.at[j, e, z], ayr.at[j, e, z], me.device(y=e))

    def a_x(j, z, e, f, src):
        return remote(src, base(j, z, e), axs.at[j, f, e, z], axr.at[j, f, e, z], me.device(x=f))

    def b_y(j, e, src):
        return remote(src, base(j, me.z), bys.at[j, e], byr.at[j, e], me.device(y=e))

    def b_x(j, e, f, src):
        return remote(src, base(j, me.z, e), bxs.at[j, e, f], bxr.at[j, e, f], me.device(x=f))

    def b_z(j, f):
        def copy(up, z, src):
            return chain(
                src, base_strip(j, z, f), bzs.at[0 if up else 1, j, f, z], bzr.at[j, f, z], up
            )

        return copy

    def core(j, f, z):
        block = base_strip(j, z, f)
        return remote(block, block, kcs.at[j, f, z], kcr.at[j, f, z], me.device(c=1))

    def give_core(j, f, z):
        if nc > 1:
            core(j, f, z).start()

    def far_z(d, visit):
        @pl.when(me.z >= d)
        def _():
            visit(me.z - d, True)

        @pl.when(me.z + d < nz)
        def _():
            visit(me.z + d, False)

    def both_ways(start, src):
        @pl.when(me.z < nz - 1)
        def _():
            start(True, me.z, src).start()

        @pl.when(me.z > 0)
        def _():
            start(False, me.z, src).start()

    def relay(copy, block, z, up):
        copy(up, z, block).wait_recv()

        @pl.when(me.z < nz - 1 if up else me.z > 0)
        def _():
            copy(up, z, block).start()

    def sent_z(start, block):
        @pl.when(me.z < nz - 1)
        def _():
            @pl.loop(0, me.z + 1)
            def _(z):
                start(True, z, block(z)).wait_send()

        @pl.when(me.z > 0)
        def _():
            @pl.loop(me.z, nz)
            def _(z):
                start(False, z, block(z)).wait_send()

    def on_wave(z, up):
        for j in range(per_owner):
            block = wave(j, z)
            relay(wave_z(j), block, z, up)
            for e in range(1, ny):
                wave_y(j, z, e, block).start()

    def on_b_y():
        keep_base.wait()
        for j in odd:
            for e in range(1, ny):
                b_y(j, e, base(j, me.z, e)).wait_recv()
                for f in range(1, nx):
                    b_x(j, e, f, base(j, me.z, e)).start()

    me.greet()
    for j in odd:
        for e in range(1, ny):
            b_y(j, e, base_ref.at[j]).start()
    for j in range(per_owner):
        both_ways(wave_z(j), wave_ref.at[j])
        for e in range(1, ny):
            wave_y(j, me.z, e, wave_ref.at[j]).start()
    for f in range(1, nx):
        for j in odd:
            b_x(j, 0, f, base_ref.at[j]).start()
        for j in even:
            a_x(j, me.z, 0, f, base_ref.at[j]).start()
    keep_wave.start()
    keep_base.start()
    for copy in take_indices:
        copy.start()
    take_left.start()
    take_right.start()
    def a_start_z():
        for j in even:
            both_ways(a_z(j), base_ref.at[j])

    def a_start_y():
        for j in even:
            for e in range(1, ny):
                a_y(j, me.z, e, base_ref.at[j]).start()

    def on_a(z, up):
        for j in even:
            block = base(j, z)
            relay(a_z(j), block, z, up)
            for e in range(1, ny):
                a_y(j, z, e, block).start()
            for f in range(1, nx):
                a_x(j, z, 0, f, block).start()

    def on_b_x(f):
        for j in odd:
            if f:
                for e in range(ny):
                    b_x(j, e, f, base(j, me.z, e, f)).wait_recv()
            block = base_strip(j, me.z, f)
            both_ways(b_z(j, f), block)
            give_core(j, f, me.z)

    def on_b(f, z, up):
        for j in odd:
            block = base_strip(j, z, f)
            relay(b_z(j, f), block, z, up)
            give_core(j, f, z)

    def on_a_y(z, up=True):
        for j in even:
            for e in range(1, ny):
                block = base(j, z, e)
                a_y(j, z, e, block).wait_recv()
                for f in range(1, nx):
                    a_x(j, z, e, f, block).start()
            give_core(j, 0, z)

    def on_a_x(z, up=True):
        for j in even:
            for f in range(1, nx):
                for e in range(ny):
                    a_x(j, z, e, f, base(j, z, e, f)).wait_recv()
                give_core(j, f, z)

    def take_wave():
        keep_wave.wait()
        for copy in take_indices:
            copy.wait()
        take_left.wait()
        take_right.wait()
        for e in range(1, ny):

            @pl.loop(0, nz)
            def _(z):
                for j in range(per_owner):
                    wave_y(j, z, e, wave(j, z, e)).wait_recv()

        row = lax.broadcasted_iota(jnp.int32, (width, width), 0)
        column = lax.broadcasted_iota(jnp.int32, (width, width), 1)
        for j in range(per_owner):
            order = order_of(first + j, sector_slot, orders, sectors)
            inside = jnp.maximum(row, column) < order
            masked[j] = jnp.where(inside, wave_all[j], jnp.zeros((), bf16))

    def multiply(p, part):
        a = lax.rem(sector_slot[source[p]], per_owner)
        block = pl.ds(pl.multiple_of(part_of(part) * (deep * strip), strip), deep * strip)
        projected = jnp.dot(left[p, block, :], masked[a], preferred_element_type=f32)
        product[p, block, :] = lax.dot_general(
            projected.astype(bf16), right[p], (((1,), (1,)), ((), ())),
            preferred_element_type=f32,
        )

    def partial_sum(slot, start, size):
        landed = [sector_slot[target[p]] for p in range(count)]
        total = None
        for p in range(count):
            weight = jnp.where(landed[p] == slot, 1.0, 0.0).astype(f32)
            term = product[p, pl.ds(start, size), :] * weight
            total = term if total is None else total + term
        return total

    def axes(j):
        return ("x", "y") if j % 2 == 0 else ("y", "x")

    def core_copy(x, j, d):
        return remote(
            send_c.at[d, j, x], got_c.at[d, j, x], cs.at[d, j, x], cr.at[d, j, x], me.device(c=1)
        )

    def copy_1(j, d, k):
        return remote(
            send_1.at[d, j, k], got_1.at[d, j, k], s1.at[d, j, k], r1.at[d, j, k],
            me.device(**{axes(j)[0]: k}),
        )

    def copy_2(j, d, k):
        return remote(
            send_2.at[d, j, k], got_2.at[d, j, k], s2.at[d, j, k], r2.at[d, j, k],
            me.device(**{axes(j)[1]: k}),
        )

    def copy_3(j, d):
        return remote(
            send_3.at[d, j], got_3.at[d, j], s3.at[d, j], r3.at[d, j],
            me.device(z=lax.rem(z_of(d) - me.z + nz, nz)),
        )

    def stage_0(d):
        @pl.loop(0, per_owner * nx)
        def _(i):
            j, x = i // nx, lax.rem(i, nx)
            slot = (x * nc + lax.rem(me.c + 1, nc)) * per_owner + j
            for m in range(ny):
                value = partial_sum(slot, pl.multiple_of(z_of(d) * strip + m * slab, slab), slab)
                send_c[d, j, x, pl.ds(m * slab, slab), :] = value.astype(bf16)
            core_copy(x, j, d).start()

    def stage_1(d):
        for j in range(per_owner):
            n1 = size[axes(j)[0]]
            n2 = size[axes(j)[1]]
            if nc > 1:
                for x in range(nx):
                    core_copy(x, j, d).wait_recv()
            for k in list(range(1, n1)) + [0]:

                for m in range(n2):
                    if axes(j)[0] == "x":
                        x, y = lax.rem(me.x + k, nx), m
                    else:
                        x, y = m, lax.rem(me.y + k, ny)
                    offset = pl.multiple_of(y * slab, slab)
                    slot = (x * nc + me.c) * per_owner + j
                    value = partial_sum(slot, pl.multiple_of(z_of(d) * strip + offset, slab), slab)
                    if nc > 1:
                        value = value + got_c[d, j, x, pl.ds(offset, slab), :].astype(f32)
                    if k:
                        send_1[d, j, k, m] = value.astype(bf16)
                    else:
                        mid[d, j, m] = value
                if k:
                    copy_1(j, d, k).start()

    def stage_2(d):
        for j in range(per_owner):
            axis_1, axis_2 = axes(j)
            n1, n2 = size[axis_1], size[axis_2]
            for k in range(1, n1):
                copy_1(j, d, k).wait_recv()
            for h in list(range(1, n2)) + [0]:
                m = lax.rem(getattr(me, axis_2) + h, n2)
                value = mid[d, j, m]
                for k in range(1, n1):
                    value = value + got_1[d, j, k, m].astype(f32)
                if h:
                    send_2[d, j, h] = value.astype(bf16)
                    copy_2(j, d, h).start()
                else:
                    held[d, j] = value

    def stage_3(d, j):
        for h in range(1, size[axes(j)[1]]):
            copy_2(j, d, h).wait_recv()
        value = held[d, j]
        for h in range(1, size[axes(j)[1]]):
            value = value + got_2[d, j, h].astype(f32)
        return value

    def stage_3_send(d):
        for j in range(per_owner):
            send_3[d, j] = stage_3(d, j).astype(bf16)
            copy_3(j, d).start()

    take_bases = pltpu.make_async_copy(
        base_all.at[pl.ds(first, per_owner)], own_bases, local.at[4]
    )

    def rotate_half():
        take_bases.start()
        take_bases.wait()
        for p in range(count):
            a = lax.rem(sector_slot[source[p]], per_owner)
            half[p] = jnp.dot(left[p], own_bases[a], preferred_element_type=f32).astype(bf16)

    def give_rotated(p):
        return pltpu.make_async_copy(right.at[p], rotated_hbm.at[p], give.at[p])

    def rotate():
        if nc > 1:
            for j in range(per_owner):
                for f in range(nx):

                    @pl.loop(0, nz)
                    def _(z):
                        core(j, f, z).wait_recv()

        for p in range(count):
            right[p] = lax.dot_general(
                base_all[sector_slot[target[p]]], half[p], (((0,), (0,)), ((), ())),
                preferred_element_type=f32,
            ).astype(bf16)
            give_rotated(p).start()

    def sent_bases():
        for j in range(per_owner):
            sent_z(wave_z(j), functools.partial(wave, j))

        @pl.loop(0, nz)
        def _(z):
            for j in range(per_owner):
                for e in range(1, ny):
                    wave_y(j, z, e, wave(j, z)).wait_send()
            for j in even:
                for e in range(1, ny):
                    a_y(j, z, e, base(j, z)).wait_send()
                for f in range(1, nx):
                    for e in range(ny):
                        a_x(j, z, e, f, base(j, z, e)).wait_send()

        for j in even:
            sent_z(a_z(j), functools.partial(base, j))
        for j in odd:
            for e in range(1, ny):
                b_y(j, e, base(j, me.z)).wait_send()
            for f in range(1, nx):
                for e in range(ny):
                    b_x(j, e, f, base(j, me.z, e)).wait_send()

    tasks = []

    def plan(key, visit, *args):
        tasks.append((key, len(tasks), visit, args))

    def after(key, *names):
        return max([key] + [done[name] for name in names])

    def step(name, d, f, needs, visit, *args):
        done[name, d, f] = after(timed(name, d, f), *needs)
        plan(done[name, d, f], visit, *args)

    done = {}
    for d in range(1, nz):
        plan(min(timed("wave", d), 0.0), far_z, d, on_wave)
    step("start_b_x", 0, 0, [], on_b_y)
    step("start_a_z", 0, 0, [], a_start_z)
    step("start_a_y", 0, 0, [("start_b_x", 0, 0)], a_start_y)
    for f in range(nx):
        step("start_b_z", 0, f, [("start_b_x", 0, 0)], on_b_x, f)
    for d in range(nz):
        before = ("a", d - 1, 0) if d > 1 else ("start_a_z", 0, 0)
        if d:
            step("a", d, 0, [before], far_z, d, on_a)
        for name, needs, visit in (
            ("a_y", ("a", d, 0) if d else ("start_a_y", 0, 0), on_a_y),
            ("a_x", ("a_y", d, 0), on_a_x),
        ):
            if d:
                step(name, d, 0, [needs], far_z, d, visit)
            else:
                step(name, d, 0, [needs], visit, me.z)
    for d in range(1, nz):
        for f in range(nx):
            before = ("b", d - 1, f) if d > 1 else ("start_b_z", 0, f)
            step("b", d, f, [before], far_z, d, functools.partial(on_b, f))
    bases = [name for name in done]
    plan(0.0, take_wave)
    for part in range(parts):
        for p in range(count):
            step("pair", p, part, [], multiply, p, part)
    for u in range(nz):
        needs = [("pair", count - 1, u // deep)]
        for name, visit in (
            ("stage_0", stage_0 if nc > 1 else None), ("stage_1", stage_1),
            ("stage_2", stage_2), ("stage_3", stage_3_send if u < nz - 1 else None),
        ):
            if visit:
                step(name, u, 0, needs + ([(name, u - 1, 0)] if u else []), visit, u)
                needs = [(name, u, 0)]
    own = [key for key in bases if key[0] in ("a_y", "b", "start_b_z") and key[2] == 0]
    step("half", 0, 0, own, rotate_half)
    step("rotate", 0, 0, bases + [("half", 0, 0)], rotate)
    for _, _, visit, args in sorted(tasks, key=lambda task: task[:2]):
        visit(*args)
    sent_bases()
    for j in odd:
        for f in range(nx):
            sent_z(b_z(j, f), lambda z: base_strip(j, z, f))
    if nc > 1:
        for j in range(per_owner):
            for f in range(nx):

                @pl.loop(0, nz)
                def _(z):
                    core(j, f, z).wait_send()

    @pl.loop(0, nz)
    def _(d):
        for j in range(per_owner):
            if nc > 1:
                for x in range(nx):
                    core_copy(x, j, d).wait_send()
            for k in range(1, size[axes(j)[0]]):
                copy_1(j, d, k).wait_send()
            for h in range(1, size[axes(j)[1]]):
                copy_2(j, d, h).wait_send()

    row = lax.broadcasted_iota(jnp.int32, (slab, width), 0) + (me.z * ny + me.y) * slab
    column = lax.broadcasted_iota(jnp.int32, (slab, width), 1)
    for j in range(per_owner):
        value = stage_3(nz - 1, j)
        for d in range(nz - 1):
            copy_3(j, d).wait_recv()
            value = value + got_3[d, j].astype(f32)
        order = order_of(first + j, sector_slot, orders, sectors)
        inside = jnp.maximum(row, column) < order
        out[j] = jnp.where(inside, value, 0.0).astype(out.dtype)

    for p in range(count):
        give_rotated(p).wait()
    @pl.loop(0, nz - 1)
    def _(d):
        for j in range(per_owner):
            copy_3(j, d).wait_send()


def sigma_and_rotation(
    dims, wavefunction, sector_bases, left, right, source, target, sector_slot, orders
):
    nx, nc, nz, ny = dims
    per_owner, slab, width = wavefunction.shape
    sectors = sector_slot.shape[0]
    most = max(nx, ny)
    dma = pltpu.SemaphoreType.DMA
    bf16, f32 = jnp.bfloat16, jnp.float32
    full = (per_owner, nz * ny * slab, width)
    return pl.pallas_call(
        functools.partial(sigma_kernel, dims, sectors),
        out_shape=(
            jax.ShapeDtypeStruct((per_owner, slab, width), bf16),
            jax.ShapeDtypeStruct(left.shape, bf16),
        ),
        in_specs=[ANY] * 8,
        out_specs=(VMEM, ANY),
        scratch_shapes=[
            pltpu.VMEM(full, bf16),
            pltpu.VMEM((sectors, nz * ny * slab, width), bf16),
            pltpu.VMEM(full, bf16),
            pltpu.VMEM(full, bf16),
            pltpu.VMEM(left.shape, bf16),
            pltpu.VMEM(left.shape, bf16),
            pltpu.VMEM(right.shape, bf16),
            pltpu.VMEM(left.shape, f32),
            pltpu.VMEM((nz, per_owner, nx, ny * slab, width), bf16),
            pltpu.VMEM((nz, per_owner, nx, ny * slab, width), bf16),
            pltpu.VMEM((nz, per_owner, most, most, slab, width), bf16),
            pltpu.VMEM((nz, per_owner, most, most, slab, width), bf16),
            pltpu.VMEM((nz, per_owner, most, slab, width), f32),
            pltpu.VMEM((nz, per_owner, most, slab, width), bf16),
            pltpu.VMEM((nz, per_owner, most, slab, width), bf16),
            pltpu.VMEM((nz, per_owner, slab, width), f32),
            pltpu.VMEM((nz, per_owner, slab, width), bf16),
            pltpu.VMEM((nz, per_owner, slab, width), bf16),
        ]
        + [dma((5,)), dma((left.shape[0],))]
        + [dma((2, per_owner, nz)), dma((per_owner, nz))]
        + [dma((per_owner, ny, nz))] * 2
        + [dma((2, per_owner, nz)), dma((per_owner, nz))]
        + [dma((per_owner, ny, nz))] * 2
        + [dma((per_owner, nx, ny, nz))] * 2
        + [dma((per_owner, ny))] * 2
        + [dma((per_owner, ny, nx))] * 2
        + [dma((2, per_owner, nx, nz)), dma((per_owner, nx, nz))]
        + [dma((per_owner, nx, nz))] * 2
        + [dma((nz, per_owner, nx))] * 2
        + [dma((nz, per_owner, most))] * 4
        + [dma((nz, per_owner))] * 2
        + [pltpu.SMEM(x.shape, x.dtype) for x in (source, target, sector_slot, orders)]
        + [dma((4,))],
        compiler_params=pltpu.CompilerParams(
            collective_id=0, has_side_effects=True, vmem_limit_bytes=60 * 1024 * 1024
        ),
        name="sigma",
    )(wavefunction, sector_bases, left, right, source, target, sector_slot, orders)


def hand_over_kernel(sigma, rotated, sigma_out, rotated_out, sigma_held, held, into, back):
    count = rotated.shape[0]

    def take(p):
        return pltpu.make_async_copy(rotated.at[p], held.at[p], into.at[p])

    def give(p):
        return pltpu.make_async_copy(held.at[p], rotated_out.at[p], back.at[p])

    take_sigma = pltpu.make_async_copy(sigma, sigma_held, into.at[count])
    give_sigma = pltpu.make_async_copy(sigma_held, sigma_out, back.at[count])
    for p in range(count):
        take(p).start()
    take_sigma.start()
    for p in range(count):
        take(p).wait()
        give(p).start()
    take_sigma.wait()
    give_sigma.start()
    for p in range(count):
        give(p).wait()
    give_sigma.wait()


def hand_over(sigma, rotated):
    count = rotated.shape[0]
    dma = pltpu.SemaphoreType.DMA
    return pl.pallas_call(
        hand_over_kernel,
        out_shape=(
            jax.ShapeDtypeStruct(sigma.shape, sigma.dtype),
            jax.ShapeDtypeStruct(rotated.shape, rotated.dtype),
        ),
        in_specs=[ANY, ANY],
        out_specs=(ANY, ANY),
        scratch_shapes=[
            pltpu.VMEM(sigma.shape, sigma.dtype),
            pltpu.VMEM(rotated.shape, rotated.dtype),
            dma((count + 1,)),
            dma((count + 1,)),
        ],
        compiler_params=pltpu.CompilerParams(vmem_limit_bytes=60 * 1024 * 1024),
        name="hand_over",
    )(sigma, rotated)


def solution(mesh):
    dims = grid_of(mesh.shape["sector"], mesh.shape["op"])

    def per_device(
        wavefunction, sector_bases, left_env, right_env, pair_source, pair_target, sector_slot, orders
    ):
        return hand_over(
            *sigma_and_rotation(
                dims, wavefunction, sector_bases, left_env, right_env,
                pair_source, pair_target, sector_slot, orders,
            )
        )

    placed = (
        P("sector", "op", None),
        P("sector", "op", None),
        P(("sector", "op"), None, None),
        P(("sector", "op"), None, None),
        P(("sector", "op")),
        P(("sector", "op")),
        P(),
        P(),
    )
    return jax.shard_map(
        per_device,
        mesh=mesh,
        in_specs=placed,
        out_specs=(P("sector", "op", None), P(("sector", "op"), None, None)),
        check_vma=False,
    )
```
